256 devices in a mesh: seq: 64 (over z, x, core), head: 4 (over y).
Axes of the slice: x: 4, y: 4, z: 8, core: 2. Of those that a mesh axis runs over, the one named last changes fastest.
Arguments:
- queries: bfloat16 [32768, 4096], P(('seq', 'head')), may hold values from -6 to 6
- keys: bfloat16 [32768, 4096], P(('seq', 'head')), may hold values from -6 to 6
- values: bfloat16 [32768, 4096], P(('seq', 'head')), may hold values from -128 to 128
- out_grad: bfloat16 [32768, 4096], P(('seq', 'head')), may hold values from -16 to 16
- doc_lengths: int32 [8], replicated, may hold values from 1 to 16384, 32768 in all
Outputs:
- attn_out: bfloat16 [32768, 4096], P(('seq', 'head'))
- grad_queries: bfloat16 [32768, 4096], P(('seq', 'head'))
- grad_keys: bfloat16 [32768, 4096], P(('seq', 'head'))
- grad_values: bfloat16 [32768, 4096], P(('seq', 'head'))
The draws below stay inside these ranges and needn't reach their ends.
Inputs may be any that keep to these rules, and one draw needn't show every extreme that they name: `doc_lengths`: the lengths sum to 32768; the longest is exactly 16384.
All inputs are finite; a program needn't handle non-finite values.
Results may differ from the reference program's by a relative error of at most 0.011.
Values may be sent and summed in bfloat16 or wider, within the bound.
A program may use at most 128 MiB of HBM per device.

```python
import math
import jax
import jax.numpy as jnp
import numpy as np
from jax import lax

H = 32
DH = 128
GROUP = 512
NDOC = 8
TOKENS = 32768
DOC_MOST = 16384
N_SEQ = 64


def draw_values(key, part):
    key_base, key_cols, key_rows = jax.random.split(key, 3)
    sample = jnp.clip(jax.random.normal(key_base, (TOKENS, H * DH), jnp.float32), -4.0, 4.0)
    log_top = math.log(10.0)
    col_scale = jnp.exp(jax.random.uniform(key_cols, (1, H * DH), jnp.float32, 0.0, log_top))
    row_scale = jnp.exp(jax.random.uniform(key_rows, (TOKENS, 1), jnp.float32, 0.0, log_top))
    return (sample * col_scale * row_scale / 8.0).astype(jnp.bfloat16)


def block_scale(own_key, extent, cuts, smallest, high):
    factor_of, own = 1.0, jax.random.fold_in(own_key, 6)
    for dim, blocks in cuts:
        heights = jnp.exp(jax.random.uniform(jax.random.fold_in(own, dim), (blocks,), jnp.float32, smallest / len(cuts), high / len(cuts)))
        factor_of = factor_of * jnp.repeat(heights, extent[dim] // blocks).reshape([-1 if axis == dim else 1 for axis in range(len(extent))])
    return factor_of


def length_profile(amount, total, bound, skew):
    portions = [(1 << 20) // math.isqrt(standing ** skew) + 1 for standing in range(2, amount + 1)]
    surplus, holding = total - bound - (amount - 1), [1] * (amount - 1)
    while surplus > 0:
        candidates = [i for i in range(amount - 1) if holding[i] < bound]
        mass, remaining = sum([portions[i] for i in candidates]), surplus
        for i in candidates:
            more = min(bound - holding[i], max(1, remaining * portions[i] // mass), surplus)
            holding[i] = holding[i] + more
            surplus = surplus - more
    return np.array([bound] + holding)


def uneven(key, amount, total, bound, skew):
    if amount == 2:
        one = jax.random.randint(key, (), max(1, total - bound), min(bound, total - 1) + 1)
        return jnp.stack([one, total - one])
    sizes = jnp.asarray(length_profile(amount, total, bound, skew), jnp.int32)
    couples = (amount - 1) // 2
    giver, receiver = sizes[1:1 + 2 * couples:2], sizes[2:2 + 2 * couples:2]
    margin = jnp.minimum(giver - 1, bound - receiver)
    moved = jax.random.randint(jax.random.fold_in(key, 1), (couples,), 0, 1 << 20) % (margin + 1)
    sizes = sizes.at[1:1 + 2 * couples:2].set(giver - moved).at[2:2 + 2 * couples:2].set(receiver + moved)
    return sizes[jax.random.permutation(jax.random.fold_in(key, 2), amount)]


def noise(rng, extent, deviation, limit, pieces=(), kind=jnp.bfloat16):
    drawn = jax.random.normal(rng, extent, jnp.float32) * deviation
    if len(pieces) > 0:
        drawn = block_scale(rng, extent, pieces, -0.22, 0.18) * drawn
    return jnp.clip(drawn, min=-limit, max=limit).astype(kind)


def setup_inputs(seed: int = 0) -> dict:
    seeds = jax.random.split(jax.random.key(seed), 6)
    queries = noise(seeds[0], (TOKENS, H * DH), 1.0, 6.0, ((0, 256),))
    keys = noise(seeds[1], (TOKENS, H * DH), 1.0, 6.0, ((0, 256),))
    values = draw_values(jax.random.fold_in(seeds[5], 71), 0)
    out_grad = noise(seeds[3], (TOKENS, H * DH), 4.0, 16.0, ((0, 256),))
    doc_lengths = uneven(seeds[4], NDOC, TOKENS, DOC_MOST, 1).astype(jnp.int32)
    return {"queries": queries, "keys": keys, "values": values, "out_grad": out_grad, "doc_lengths": doc_lengths}


def feature(array):
    wide = array.astype(jnp.float32)
    return jnp.where(wide > 0, wide + 1.0, jnp.exp(jnp.minimum(wide, 0.0)))

def slope(array):
    wide = array.astype(jnp.float32)
    return jnp.where(wide > 0, 1.0, jnp.exp(jnp.minimum(wide, 0.0)))

def doc_index(doc_ends, where):
    return lax.optimization_barrier(jnp.sum((where[..., None] >= doc_ends).astype(jnp.int32), axis=-1))

def reference(queries, keys, values, out_grad, doc_lengths):
    doc_ends = jnp.cumsum(doc_lengths).astype(jnp.int32)
    within = jnp.arange(GROUP, dtype=jnp.int32)
    causal = within[:, None] >= within[None, :]

    def blocked(array):
        return array.reshape(N_SEQ, GROUP, H, DH)
    query_all = blocked(queries)
    key_all = blocked(keys)
    value_all = blocked(values)
    grad_all = blocked(out_grad)
    block_ids = jnp.arange(N_SEQ, dtype=jnp.int32)

    def layout(block_index):
        block_start = block_index * GROUP
        doc_of = doc_index(doc_ends, block_start + within)
        doc_first = doc_of[0]
        doc_last = doc_of[GROUP - 1]
        before = doc_index(doc_ends, block_start - 1)
        doc_after = doc_index(doc_ends, block_start + GROUP)
        visible = causal & (doc_of[:, None] == doc_of[None, :])
        head_rows = (doc_of == doc_first).astype(jnp.float32)[:, None, None]
        tail_rows = (doc_of == doc_last).astype(jnp.float32)[:, None, None]
        return (doc_first, doc_last, before, doc_after, visible, head_rows, tail_rows)

    def forward_part(query_blk, key_blk, value_blk, incoming, visible, head_rows):
        feat_query = feature(query_blk).astype(jnp.bfloat16)
        feat_key = feature(key_blk).astype(jnp.bfloat16)
        scores = jnp.einsum('thd,shd->hts', feat_query.astype(jnp.float32), feat_key.astype(jnp.float32))
        scores = jnp.where(visible[None], scores, 0.0).astype(jnp.bfloat16)
        carried_term = jnp.einsum('thd,hde->the', feat_query.astype(jnp.float32), incoming.astype(jnp.float32)) * head_rows
        attended = carried_term + jnp.einsum('hts,she->the', scores.astype(jnp.float32), value_blk.astype(jnp.float32))
        inv_rms = lax.rsqrt(lax.optimization_barrier(jnp.mean(attended * attended, axis=-1, keepdims=True)) + 1e-05)
        normed = attended * inv_rms
        return (feat_query, feat_key, scores, inv_rms, normed)

    def forward_step(state, members):
        block_index, query_blk, key_blk, value_blk = members
        doc_first, doc_last, before, doc_after, visible, head_rows, tail_rows = layout(block_index)
        incoming = jnp.where(doc_first == before, state, 0.0).astype(jnp.bfloat16)
        feat_query, feat_key, scores, inv_rms, normed = forward_part(query_blk, key_blk, value_blk, incoming, visible, head_rows)
        tail_state = jnp.einsum('shd,she->hde', feat_key.astype(jnp.float32) * tail_rows, value_blk.astype(jnp.float32))
        new_state = jnp.where(doc_last == before, state, 0.0) + tail_state
        return (new_state, (incoming, normed.astype(jnp.bfloat16)))
    zero_state = jnp.zeros((H, DH, DH), jnp.float32)
    _, (incomings, outputs) = lax.scan(forward_step, zero_state, (block_ids, query_all, key_all, value_all))

    def backward_step(state, members):
        block_index, query_blk, key_blk, value_blk, grad_blk, incoming = members
        doc_first, doc_last, before, doc_after, visible, head_rows, tail_rows = layout(block_index)
        feat_query, feat_key, scores, inv_rms, normed = forward_part(query_blk, key_blk, value_blk, incoming, visible, head_rows)
        grad_out = grad_blk.astype(jnp.float32)
        grad_att = ((grad_out - normed * lax.optimization_barrier(jnp.mean(grad_out * normed, axis=-1, keepdims=True))) * inv_rms).astype(jnp.bfloat16)
        outgoing = jnp.where(doc_last == doc_after, state, 0.0).astype(jnp.bfloat16)
        fq32 = feat_query.astype(jnp.float32)
        fk32 = feat_key.astype(jnp.float32)
        value32 = value_blk.astype(jnp.float32)
        ga32 = grad_att.astype(jnp.float32)
        grad_scores = jnp.einsum('the,she->hts', ga32, value32)
        grad_scores = jnp.where(visible[None], grad_scores, 0.0).astype(jnp.bfloat16).astype(jnp.float32)
        grad_fq = jnp.einsum('hts,shd->thd', grad_scores, fk32) + jnp.einsum('the,hde->thd', ga32, incoming.astype(jnp.float32)) * head_rows
        grad_fk = jnp.einsum('hts,thd->shd', grad_scores, fq32) + jnp.einsum('she,hde->shd', value32, outgoing.astype(jnp.float32)) * tail_rows
        grad_fv = jnp.einsum('hts,the->she', scores.astype(jnp.float32), ga32) + jnp.einsum('shd,hde->she', fk32, outgoing.astype(jnp.float32)) * tail_rows
        head_sum = jnp.einsum('thd,the->hde', fq32 * head_rows, ga32)
        new_state = jnp.where(doc_first == doc_after, state, 0.0) + head_sum
        grad_query = (grad_fq * slope(query_blk)).astype(jnp.bfloat16)
        grad_key = (grad_fk * slope(key_blk)).astype(jnp.bfloat16)
        return (new_state, (grad_query, grad_key, grad_fv.astype(jnp.bfloat16)))
    _, (grad_query_all, grad_key_all, grad_value_all) = lax.scan(backward_step, zero_state, (block_ids, query_all, key_all, value_all, grad_all, incomings), reverse=True)
    width = H * DH
    return (outputs.reshape(TOKENS, width), grad_query_all.reshape(TOKENS, width), grad_key_all.reshape(TOKENS, width), grad_value_all.reshape(TOKENS, width))
```

```python
import functools

import jax
import jax.numpy as jnp
from jax import lax
from jax.experimental import pallas as pl
from jax.experimental.pallas import tpu as pltpu
from jax.sharding import PartitionSpec as P

DH = 128
DOC_MOST = 16384
UNROLL = 4
MESH = pl.DeviceIdType.MESH
F32 = jnp.float32
BF16 = jnp.bfloat16


def mm(a, b, ca, cb):
    return lax.dot_general(a, b, (((ca,), (cb,)), ((), ())), preferred_element_type=F32)


def feature(x):
    return jnp.where(x > 0, x + 1.0, jnp.exp(jnp.minimum(x, 0.0)))


def slope(x):
    return jnp.where(x > 0, 1.0, jnp.exp(jnp.minimum(x, 0.0)))


def kernel(
    cfg,
    len_ref,
    q_hbm,
    k_hbm,
    v_hbm,
    g_hbm,
    o_hbm,
    gq_hbm,
    gk_hbm,
    gv_hbm,
    q_ref,
    k_ref,
    v_ref,
    g_ref,
    o_ref,
    gq_ref,
    gk_ref,
    gv_ref,
    fq_ref,
    fk_ref,
    sc_ref,
    ga_ref,
    att_ref,
    gfk_ref,
    gfv_ref,
    state_out,
    state_in,
    total_out,
    total_in,
    visible_ref,
    rows_ref,
    weight_ref,
    send_sem,
    recv_sem,
    zsend_sem,
    zrecv_sem,
    load_sem,
):
    heads, plane_seq, head_axis, planes, reach = cfg
    groups = heads // UNROLL
    seq = lax.axis_index("seq")
    place = lax.axis_index("head")
    z = seq // plane_seq
    mine = (seq % plane_seq) * head_axis + place
    block = z * heads + mine

    def peer(p):
        return (z * plane_seq + p // head_axis, p % head_axis)

    def plane_peer(other):
        return (other * plane_seq + seq % plane_seq, place)

    def cols(h):
        return pl.ds(pl.multiple_of(h * DH, DH), DH)

    loads = [
        pltpu.make_async_copy(src, dst, load_sem.at[n])
        for n, (src, dst) in enumerate(
            ((k_hbm, k_ref), (v_hbm, v_ref), (q_hbm, q_ref), (g_hbm, g_ref))
        )
    ]
    for load in loads:
        load.start()

    barrier = pltpu.get_barrier_semaphore()

    def greet(n, carry):
        pl.semaphore_signal(
            barrier, inc=1, device_id=peer((mine + n) % heads), device_id_type=MESH
        )
        return carry

    lax.fori_loop(1, heads, greet, 0)
    for n in range(1, planes):
        pl.semaphore_signal(
            barrier, inc=1, device_id=plane_peer((z + n) % planes), device_id_type=MESH
        )

    ends = []
    end = jnp.int32(0)
    for n in range(len_ref.shape[0]):
        end = end + len_ref[n]
        ends.append(end)

    def doc_of(where):
        return sum([(where >= e).astype(jnp.int32) for e in ends])

    def equal(a, b):
        return jnp.where(a == b, 1.0, 0.0).astype(F32)

    start = block * DH
    row_doc = doc_of(start + lax.broadcasted_iota(jnp.int32, (DH, DH), 0))
    col_doc = doc_of(start + lax.broadcasted_iota(jnp.int32, (DH, DH), 1))
    causal = lax.broadcasted_iota(jnp.int32, (DH, DH), 0) >= lax.broadcasted_iota(
        jnp.int32, (DH, DH), 1
    )
    visible_ref[...] = jnp.where(causal & (row_doc == col_doc), 1.0, 0.0).astype(F32)
    rows_ref[0] = jnp.where(row_doc == doc_of(start), 1.0, 0.0).astype(F32)
    rows_ref[1] = jnp.where(row_doc == doc_of(start + DH - 1), 1.0, 0.0).astype(F32)

    plane_start = z * (heads * DH)
    plane_first = doc_of(plane_start)
    plane_last = doc_of(plane_start + heads * DH - 1)

    def weigh(i, carry):
        begin = plane_start + i * DH
        before, first = doc_of(begin - 1), doc_of(begin)
        last, after = doc_of(begin + DH - 1), doc_of(begin + DH)
        weight_ref[0, i] = equal(last, plane_last)
        weight_ref[1, i] = equal(last, before)
        weight_ref[2, i] = equal(first, before)
        weight_ref[3, i] = equal(first, plane_first)
        weight_ref[4, i] = equal(first, after)
        weight_ref[5, i] = equal(last, after)
        return carry

    lax.fori_loop(0, heads, weigh, 0)

    def remote(stage, slot, target_slot, p):
        return pltpu.make_async_remote_copy(
            src_ref=state_out.at[stage, slot],
            dst_ref=state_in.at[stage, target_slot],
            send_sem=send_sem.at[stage, slot],
            recv_sem=recv_sem.at[stage, target_slot],
            device_id=peer(p),
            device_id_type=MESH,
        )

    def send(stage, p):
        remote(stage, p, mine, p).start()

    def receive(stage, p):
        remote(stage, p, p, p).wait_recv()

    def to_own(stage):
        state_in[stage, mine] = state_out[stage, mine]

    def forward_state(kk):
        h = (mine + kk) % heads
        fk = feature(k_ref[:, cols(h)].astype(F32))
        fk_ref[h] = fk.astype(BF16)
        masked = (fk * rows_ref[1]).astype(BF16)
        state_out[0, h] = mm(masked, v_ref[:, cols(h)], 0, 0).astype(BF16)

    loads[0].wait()
    loads[1].wait()
    for j in range(UNROLL):
        forward_state(1 + j)
    pl.semaphore_wait(barrier, heads - 1 + planes - 1)

    def forward_lap(it, carry):
        for j in range(UNROLL):
            send(0, (mine + it * UNROLL + 1 + j) % heads)
        for j in range(UNROLL):
            forward_state((it + 1) * UNROLL + 1 + j)
        return carry

    lax.fori_loop(0, groups - 1, forward_lap, 0)
    for j in range(UNROLL - 1):
        send(0, (mine + (groups - 1) * UNROLL + 1 + j) % heads)
    to_own(0)

    loads[2].wait()

    def local_lap(it, carry):
        for j in range(UNROLL):
            h = it * UNROLL + j
            fq = feature(q_ref[:, cols(h)].astype(F32)).astype(BF16)
            fq_ref[h] = fq
            scores = (mm(fq, fk_ref[h], 1, 1) * visible_ref[...]).astype(BF16)
            sc_ref[h] = scores
            att_ref[h] = mm(scores, v_ref[:, cols(h)], 1, 0)
        return carry

    lax.fori_loop(0, groups, local_lap, 0)
    loads[3].wait()

    def owner(stage, back):
        kind = 3 if back else 0

        def gather(n, total):
            i = (mine - n) % heads if not back else (mine + n) % heads

            @pl.when(n > 0)
            def _():
                receive(stage, i)

            return total + state_in[stage, i].astype(F32) * weight_ref[kind, i]

        total = lax.fori_loop(0, heads, gather, jnp.zeros((DH, DH), F32))
        total_out[back] = total.astype(BF16)
        copies = []
        for n in range(1, reach + 1):
            target = (z + n) % planes if not back else (z + planes - n) % planes
            copy = pltpu.make_async_remote_copy(
                src_ref=total_out.at[back],
                dst_ref=total_in.at[back, n - 1],
                send_sem=zsend_sem.at[back, n - 1],
                recv_sem=zrecv_sem.at[back, n - 1],
                device_id=plane_peer(target),
                device_id_type=MESH,
            )
            copy.start()
            copies.append(copy)
        carry = jnp.zeros((DH, DH), F32)
        for n in range(1, reach + 1):
            copies[n - 1].wait_recv()
            if not back:
                source = z - n
                inside = source >= 0
                doc = doc_of((source + 1) * (heads * DH) - 1)
                near = doc_of(plane_start - 1)
            else:
                source = z + n
                inside = source < planes
                doc = doc_of(source * (heads * DH))
                near = doc_of(plane_start + heads * DH)
            scale = jnp.where(inside, equal(doc, near), 0.0)
            carry = carry + total_in[back, n - 1].astype(F32) * scale

        def scan(n, run):
            i = n if not back else heads - 1 - n
            state_out[stage + 1, i] = (run * weight_ref[kind + 2, i]).astype(BF16)
            return state_in[stage, i].astype(F32) + run * weight_ref[kind + 1, i]

        lax.fori_loop(0, heads, scan, carry)

        def spread(n, c):
            send(stage + 1, (mine + n) % heads)
            return c

        lax.fori_loop(1, heads, spread, 0)
        to_own(stage + 1)
        return copies

    forward_copies = owner(0, 0)

    def attend(kk):
        h = (mine + heads - kk) % heads
        head_rows = rows_ref[0]
        fq = fq_ref[h]
        att = att_ref[h] + mm(fq, state_in[1, h], 1, 0) * head_rows
        inv = lax.rsqrt(jnp.mean(att * att, axis=-1, keepdims=True) + 1e-05)
        normed = att * inv
        o_ref[:, cols(h)] = normed.astype(BF16)
        grad = g_ref[:, cols(h)].astype(F32)
        ga = ((grad - normed * jnp.mean(grad * normed, axis=-1, keepdims=True)) * inv).astype(BF16)
        ga_ref[h] = ga
        masked = (fq.astype(F32) * head_rows).astype(BF16)
        state_out[2, h] = mm(masked, ga, 0, 0).astype(BF16)

    def attend_lap(it, carry):
        for j in range(UNROLL):
            kk = it * UNROLL + j

            @pl.when(kk > 0)
            def _():
                receive(1, (mine + heads - kk) % heads)

        for j in range(UNROLL):
            attend(it * UNROLL + j)
        for j in range(UNROLL):
            kk = it * UNROLL + j

            @pl.when(kk > 0)
            def _():
                send(2, (mine + heads - kk) % heads)

        return carry

    lax.fori_loop(0, groups, attend_lap, 0)
    to_own(2)
    store_out = pltpu.make_async_copy(o_ref, o_hbm, load_sem.at[4])
    store_out.start()

    def local_back(it, carry):
        for j in range(UNROLL):
            h = it * UNROLL + j
            ga, fq, fk = ga_ref[h], fq_ref[h], fk_ref[h]
            grads = (mm(ga, v_ref[:, cols(h)], 1, 1) * visible_ref[...]).astype(BF16)
            gfq = mm(grads, fk, 1, 0) + mm(ga, state_in[1, h], 1, 1) * rows_ref[0]
            gq_ref[:, cols(h)] = (gfq * slope(q_ref[:, cols(h)].astype(F32))).astype(BF16)
            gfk_ref[h] = mm(grads, fq, 0, 0)
            gfv_ref[h] = mm(sc_ref[h], ga, 0, 0)
        return carry

    lax.fori_loop(0, groups, local_back, 0)
    store_gq = pltpu.make_async_copy(gq_ref, gq_hbm, load_sem.at[5])
    store_gq.start()

    back_copies = owner(2, 1)

    def finish(it, carry):
        for j in range(UNROLL):
            kk = it * UNROLL + j

            @pl.when(kk > 0)
            def _():
                receive(3, (mine + heads - kk) % heads)

        for j in range(UNROLL):
            h = (mine + heads - (it * UNROLL + j)) % heads
            outgoing = state_in[3, h]
            gfk = gfk_ref[h] + mm(v_ref[:, cols(h)], outgoing, 1, 1) * rows_ref[1]
            gk_ref[:, cols(h)] = (gfk * slope(k_ref[:, cols(h)].astype(F32))).astype(BF16)
            gfv = gfv_ref[h] + mm(fk_ref[h], outgoing, 1, 0) * rows_ref[1]
            gv_ref[:, cols(h)] = gfv.astype(BF16)
        return carry

    lax.fori_loop(0, groups, finish, 0)
    store_gk = pltpu.make_async_copy(gk_ref, gk_hbm, load_sem.at[6])
    store_gv = pltpu.make_async_copy(gv_ref, gv_hbm, load_sem.at[7])
    store_gk.start()
    store_gv.start()

    def drain(n, carry):
        p = (mine + n) % heads
        for stage in range(4):
            remote(stage, p, mine, p).wait_send()
        return carry

    lax.fori_loop(1, heads, drain, 0)
    for copy in forward_copies + back_copies:
        copy.wait_send()
    store_out.wait()
    store_gq.wait()
    store_gk.wait()
    store_gv.wait()


def solution(mesh):
    seq_axis, head_axis = mesh.shape["seq"], mesh.shape["head"]

    def local(queries, keys, values, out_grad, doc_lengths):
        rows, width = queries.shape
        heads = width // DH
        plane_seq = heads // head_axis
        planes = seq_axis // plane_seq
        reach = min(planes - 1, -(-DOC_MOST // (heads * DH)))
        cfg = (heads, plane_seq, head_axis, planes, reach)
        flat = [pltpu.VMEM((rows, width), BF16)] * 8
        per_head = [pltpu.VMEM((heads, DH, DH), BF16)] * 4
        wide = [pltpu.VMEM((heads, DH, DH), F32)] * 3
        out = jax.ShapeDtypeStruct((rows, width), BF16)
        hbm = pl.BlockSpec(memory_space=pl.ANY)
        return pl.pallas_call(
            functools.partial(kernel, cfg),
            out_shape=(out,) * 4,
            in_specs=[pl.BlockSpec(memory_space=pltpu.SMEM)] + [hbm] * 4,
            out_specs=(hbm,) * 4,
            scratch_shapes=flat
            + per_head
            + wide
            + [
                pltpu.VMEM((4, heads, DH, DH), BF16),
                pltpu.VMEM((4, heads, DH, DH), BF16),
                pltpu.VMEM((2, DH, DH), BF16),
                pltpu.VMEM((2, reach, DH, DH), BF16),
                pltpu.VMEM((DH, DH), F32),
                pltpu.VMEM((2, DH, DH), F32),
                pltpu.SMEM((6, heads), F32),
                pltpu.SemaphoreType.DMA((4, heads)),
                pltpu.SemaphoreType.DMA((4, heads)),
                pltpu.SemaphoreType.DMA((2, reach)),
                pltpu.SemaphoreType.DMA((2, reach)),
                pltpu.SemaphoreType.DMA((8,)),
            ],
            compiler_params=pltpu.CompilerParams(
                collective_id=0, has_side_effects=True, vmem_limit_bytes=56 << 20
            ),
        )(doc_lengths, queries, keys, values, out_grad)

    return jax.shard_map(
        local,
        mesh=mesh,
        in_specs=(P(("seq", "head"), None),) * 4 + (P(),),
        out_specs=(P(("seq", "head"), None),) * 4,
        check_vma=False,
    )
```

```python
import functools

import jax
import jax.numpy as jnp
from jax import lax
from jax.experimental import pallas as pl
from jax.experimental.pallas import tpu as pltpu
from jax.sharding import PartitionSpec as P

DH = 128
DOC_MOST = 16384
UNROLL = 4
GROUPS = 4
MESH = pl.DeviceIdType.MESH
F32 = jnp.float32
BF16 = jnp.bfloat16


def mm(a, b, ca, cb):
    return lax.dot_general(a, b, (((ca,), (cb,)), ((), ())), preferred_element_type=F32)


def feature(x):
    return jnp.where(x > 0, x + 1.0, jnp.exp(jnp.minimum(x, 0.0)))


def slope(x):
    return jnp.where(x > 0, 1.0, jnp.exp(jnp.minimum(x, 0.0)))


def kernel(
    cfg,
    len_ref,
    q_hbm,
    k_hbm,
    v_hbm,
    g_hbm,
    o_hbm,
    gq_hbm,
    gk_hbm,
    gv_hbm,
    q_ref,
    k_ref,
    v_ref,
    g_ref,
    o_ref,
    gq_ref,
    gk_ref,
    gv_ref,
    fq_ref,
    fk_ref,
    sc_ref,
    ga_ref,
    att_ref,
    gfk_ref,
    gfv_ref,
    state_out,
    state_in,
    prefix_out,
    prefix_in,
    total_out,
    total_in,
    visible_ref,
    rows_ref,
    weight_ref,
    send_sem,
    state_sem,
    prefix_sem,
    zsend_sem,
    zrecv_sem,
    load_sem,
):
    heads, plane_seq, head_axis, planes, reach = cfg
    per_group = heads // GROUPS
    laps = per_group // UNROLL
    slab = DH // GROUPS
    seq = lax.axis_index("seq")
    place = lax.axis_index("head")
    z = seq // plane_seq
    mine = (seq % plane_seq) * head_axis + place
    block = z * heads + mine

    def peer(p):
        return (z * plane_seq + p // head_axis, p % head_axis)

    def plane_peer(other):
        return (other * plane_seq + seq % plane_seq, place)

    def cols(h):
        return pl.ds(pl.multiple_of(h * DH, DH), DH)

    loads = [
        pltpu.make_async_copy(src, dst, load_sem.at[n])
        for n, (src, dst) in enumerate(
            ((k_hbm, k_ref), (v_hbm, v_ref), (q_hbm, q_ref), (g_hbm, g_ref))
        )
    ]
    for load in loads:
        load.start()

    barrier = pltpu.get_barrier_semaphore()

    def greet(n, carry):
        pl.semaphore_signal(
            barrier, inc=1, device_id=peer((mine + n) % heads), device_id_type=MESH
        )
        return carry

    lax.fori_loop(1, heads, greet, 0)
    for n in range(1, planes):
        pl.semaphore_signal(
            barrier, inc=1, device_id=plane_peer((z + n) % planes), device_id_type=MESH
        )

    ends = []
    end = jnp.int32(0)
    for n in range(len_ref.shape[0]):
        end = end + len_ref[n]
        ends.append(end)

    def doc_of(where):
        return sum([(where >= e).astype(jnp.int32) for e in ends])

    def equal(a, b):
        return jnp.where(a == b, 1.0, 0.0).astype(F32)

    start = block * DH
    row_doc = doc_of(start + lax.broadcasted_iota(jnp.int32, (DH, DH), 0))
    col_doc = doc_of(start + lax.broadcasted_iota(jnp.int32, (DH, DH), 1))
    causal = lax.broadcasted_iota(jnp.int32, (DH, DH), 0) >= lax.broadcasted_iota(
        jnp.int32, (DH, DH), 1
    )
    visible_ref[...] = jnp.where(causal & (row_doc == col_doc), 1.0, 0.0).astype(F32)
    rows_ref[0] = jnp.where(row_doc == doc_of(start), 1.0, 0.0).astype(F32)
    rows_ref[1] = jnp.where(row_doc == doc_of(start + DH - 1), 1.0, 0.0).astype(F32)

    plane_start = z * (heads * DH)
    plane_first = doc_of(plane_start)
    plane_last = doc_of(plane_start + heads * DH - 1)

    def weigh(i, carry):
        begin = plane_start + i * DH
        before, first = doc_of(begin - 1), doc_of(begin)
        last, after = doc_of(begin + DH - 1), doc_of(begin + DH)
        weight_ref[0, i] = equal(last, plane_last)
        weight_ref[1, i] = equal(last, before)
        weight_ref[2, i] = equal(first, before)
        weight_ref[3, i] = equal(first, plane_first)
        weight_ref[4, i] = equal(first, after)
        weight_ref[5, i] = equal(last, after)
        return carry

    lax.fori_loop(0, heads, weigh, 0)

    def owned(g):
        return g * per_group + mine // GROUPS

    def slab_rows(s):
        return pl.ds(pl.multiple_of(s * slab, slab), slab)

    def state_copy(way, g, p):
        source = state_out.at[way, g * per_group + p // GROUPS, slab_rows(p % GROUPS)]
        return source, state_in.at[way, g, mine], state_sem.at[way, g]

    def prefix_copy(way, g, p):
        target = prefix_in.at[way, owned(g), slab_rows(mine % GROUPS)]
        return prefix_out.at[way, g, p], target, prefix_sem.at[way, owned(g)]

    def remote(refs, sem, p):
        return pltpu.make_async_remote_copy(
            src_ref=refs[0],
            dst_ref=refs[1],
            send_sem=sem,
            recv_sem=refs[2],
            device_id=peer(p),
            device_id_type=MESH,
        )

    def dispatch(refs, sem, p):
        own = p == mine

        @pl.when(own)
        def _():
            pltpu.make_async_copy(*refs).start()

        @pl.when(jnp.logical_not(own))
        def _():
            remote(refs, sem, p).start()

    def send_states(way, g, a):
        for s in range(GROUPS):
            p = a * GROUPS + (mine + s) % GROUPS
            dispatch(state_copy(way, g, p), send_sem.at[way, 0], p)

    def ahead(it, j):
        g, lap = it // laps, it % laps
        return g, (mine // GROUPS + lap * UNROLL + j) % per_group

    def forward_lap(it, carry):
        @pl.when(it < GROUPS * laps)
        def _():
            for j in range(UNROLL):
                g, a = ahead(it, j)
                h = g * per_group + a
                fk = feature(k_ref[:, cols(h)].astype(F32))
                fk_ref[h] = fk.astype(BF16)
                masked = (fk * rows_ref[1]).astype(BF16)
                state_out[0, h] = mm(masked, v_ref[:, cols(h)], 0, 0).astype(BF16)

        @pl.when(it == 1)
        def _():
            pl.semaphore_wait(barrier, heads - 1 + planes - 1)

        @pl.when(it > 0)
        def _():
            for j in range(UNROLL):
                g, a = ahead(it - 1, j)
                send_states(0, g, a)

        return carry

    def local_forward(g):
        def lap(it, carry):
            for j in range(UNROLL):
                h = g * per_group + it * UNROLL + j
                fq = feature(q_ref[:, cols(h)].astype(F32)).astype(BF16)
                fq_ref[h] = fq
                scores = (mm(fq, fk_ref[h], 1, 1) * visible_ref[...]).astype(BF16)
                sc_ref[h] = scores
                att_ref[h] = mm(scores, v_ref[:, cols(h)], 1, 0)
            return carry

        lax.fori_loop(0, laps, lap, 0)

    def total_copy(way, g, n):
        target = (z + n) % planes if way == 0 else (z + planes - n) % planes
        return pltpu.make_async_remote_copy(
            src_ref=total_out.at[way, g],
            dst_ref=total_in.at[way, g, n - 1],
            send_sem=zsend_sem.at[way],
            recv_sem=zrecv_sem.at[way, g, n - 1],
            device_id=plane_peer(target),
            device_id_type=MESH,
        )

    def sum_up(way, g):
        pltpu.make_async_copy(state_in.at[way, g], state_in.at[way, g], state_sem.at[way, g]).wait()

        def add(n, total):
            for j in range(4):
                i = n * 4 + j
                total = total + state_in[way, g, i].astype(F32) * weight_ref[3 * way, i]
            return total

        total = lax.fori_loop(0, heads // 4, add, jnp.zeros((slab, DH), F32))
        total_out[way, g] = total.astype(BF16)
        for n in range(1, reach + 1):
            total_copy(way, g, n).start()

    def scan(way, g):
        run = jnp.zeros((slab, DH), F32)
        for n in range(1, reach + 1):
            total_copy(way, g, n).wait_recv()
            if way == 0:
                source = z - n
                inside = source >= 0
                doc = doc_of((source + 1) * (heads * DH) - 1)
                near = doc_of(plane_start - 1)
            else:
                source = z + n
                inside = source < planes
                doc = doc_of(source * (heads * DH))
                near = doc_of(plane_start + heads * DH)
            scale = jnp.where(inside, equal(doc, near), 0.0)
            run = run + total_in[way, g, n - 1].astype(F32) * scale

        def step(n, run):
            for j in range(4):
                i = n * 4 + j
                i = i if way == 0 else heads - 1 - i
                prefix_out[way, g, i] = (run * weight_ref[3 * way + 2, i]).astype(BF16)
                run = state_in[way, g, i].astype(F32) + run * weight_ref[3 * way + 1, i]
            return run

        lax.fori_loop(0, heads // 4, step, run)

        def spread(n, carry):
            p = (mine + n) % heads
            dispatch(prefix_copy(way, g, p), send_sem.at[way, 1], p)
            return carry

        lax.fori_loop(0, heads, spread, 0)

    def arrive(way, h):
        pltpu.make_async_copy(prefix_in.at[way, h], prefix_in.at[way, h], prefix_sem.at[way, h]).wait()

    def behind(it, j):
        g, lap = it // laps, it % laps
        return g, (mine // GROUPS + per_group - lap * UNROLL - j) % per_group

    def attend_lap(it, carry):
        @pl.when(it < GROUPS * laps)
        def _():
            spots = [behind(it, j) for j in range(UNROLL)]
            for g, a in spots:
                arrive(0, g * per_group + a)
            for g, a in spots:
                h = g * per_group + a
                head_rows = rows_ref[0]
                fq = fq_ref[h]
                att = att_ref[h] + mm(fq, prefix_in[0, h], 1, 0) * head_rows
                inv = lax.rsqrt(jnp.mean(att * att, axis=-1, keepdims=True) + 1e-05)
                normed = att * inv
                o_ref[:, cols(h)] = normed.astype(BF16)
                grad = g_ref[:, cols(h)].astype(F32)
                mean = jnp.mean(grad * normed, axis=-1, keepdims=True)
                ga = ((grad - normed * mean) * inv).astype(BF16)
                ga_ref[h] = ga
                masked = (fq.astype(F32) * head_rows).astype(BF16)
                state_out[1, h] = mm(masked, ga, 0, 0).astype(BF16)

        @pl.when(it > 0)
        def _():
            for j in range(UNROLL):
                g, a = behind(it - 1, j)
                send_states(1, g, a)

        return carry

    def local_back(g):
        def lap(it, carry):
            for j in range(UNROLL):
                h = g * per_group + it * UNROLL + j
                ga, fq, fk = ga_ref[h], fq_ref[h], fk_ref[h]
                grads = (mm(ga, v_ref[:, cols(h)], 1, 1) * visible_ref[...]).astype(BF16)
                gfq = mm(grads, fk, 1, 0) + mm(ga, prefix_in[0, h], 1, 1) * rows_ref[0]
                gq_ref[:, cols(h)] = (gfq * slope(q_ref[:, cols(h)].astype(F32))).astype(BF16)
                gfk_ref[h] = mm(grads, fq, 0, 0)
                gfv_ref[h] = mm(sc_ref[h], ga, 0, 0)
            return carry

        lax.fori_loop(0, laps, lap, 0)

    def finish(it, carry):
        spots = [behind(it, j) for j in range(UNROLL)]
        for g, a in spots:
            arrive(1, g * per_group + a)
        for g, a in spots:
            h = g * per_group + a
            outgoing = prefix_in[1, h]
            gfk = gfk_ref[h] + mm(v_ref[:, cols(h)], outgoing, 1, 1) * rows_ref[1]
            gk_ref[:, cols(h)] = (gfk * slope(k_ref[:, cols(h)].astype(F32))).astype(BF16)
            gfv = gfv_ref[h] + mm(fk_ref[h], outgoing, 1, 0) * rows_ref[1]
            gv_ref[:, cols(h)] = gfv.astype(BF16)
        return carry

    def each_group(way, local, g, carry):
        local(g)
        sum_up(way, g)
        return carry

    def each_scan(way, g, carry):
        scan(way, g)
        return carry

    stores = [
        pltpu.make_async_copy(src, dst, load_sem.at[4 + n])
        for n, (src, dst) in enumerate(
            ((o_ref, o_hbm), (gq_ref, gq_hbm), (gk_ref, gk_hbm), (gv_ref, gv_hbm))
        )
    ]
    loads[0].wait()
    loads[1].wait()
    lax.fori_loop(0, GROUPS * laps + 1, forward_lap, 0)
    loads[2].wait()
    lax.fori_loop(0, GROUPS, functools.partial(each_group, 0, local_forward), 0)
    lax.fori_loop(0, GROUPS, functools.partial(each_scan, 0), 0)
    loads[3].wait()
    lax.fori_loop(0, GROUPS * laps + 1, attend_lap, 0)
    stores[0].start()
    lax.fori_loop(0, GROUPS, functools.partial(each_group, 1, local_back), 0)
    stores[1].start()
    lax.fori_loop(0, GROUPS, functools.partial(each_scan, 1), 0)
    lax.fori_loop(0, GROUPS * laps, finish, 0)
    stores[2].start()
    stores[3].start()

    for way in range(2):
        for n in range(2):
            sent = state_out.at[way, pl.ds(0, heads - 1)]
            pltpu.make_async_copy(sent, sent, send_sem.at[way, n]).wait()
        for n in range(1, reach + 1):
            pltpu.make_async_copy(total_out.at[way], total_out.at[way], zsend_sem.at[way]).wait()
    for store in stores:
        store.wait()


def solution(mesh):
    seq_axis, head_axis = mesh.shape["seq"], mesh.shape["head"]

    def local(queries, keys, values, out_grad, doc_lengths):
        rows, width = queries.shape
        heads = width // DH
        plane_seq = heads // head_axis
        planes = seq_axis // plane_seq
        reach = min(planes - 1, -(-DOC_MOST // (heads * DH)))
        cfg = (heads, plane_seq, head_axis, planes, reach)
        flat = [pltpu.VMEM((rows, width), BF16)] * 8
        per_head = [pltpu.VMEM((heads, DH, DH), BF16)] * 4
        wide = [pltpu.VMEM((heads, DH, DH), F32)] * 3
        out = jax.ShapeDtypeStruct((rows, width), BF16)
        hbm = pl.BlockSpec(memory_space=pl.ANY)
        return pl.pallas_call(
            functools.partial(kernel, cfg),
            out_shape=(out,) * 4,
            in_specs=[pl.BlockSpec(memory_space=pltpu.SMEM)] + [hbm] * 4,
            out_specs=(hbm,) * 4,
            scratch_shapes=flat
            + per_head
            + wide
            + [
                pltpu.VMEM((2, heads, DH, DH), BF16),
                pltpu.VMEM((2, GROUPS, heads, DH // GROUPS, DH), BF16),
                pltpu.VMEM((2, GROUPS, heads, DH // GROUPS, DH), BF16),
                pltpu.VMEM((2, heads, DH, DH), BF16),
                pltpu.VMEM((2, GROUPS, DH // GROUPS, DH), BF16),
                pltpu.VMEM((2, GROUPS, reach, DH // GROUPS, DH), BF16),
                pltpu.VMEM((DH, DH), F32),
                pltpu.VMEM((2, DH, DH), F32),
                pltpu.SMEM((6, heads), F32),
                pltpu.SemaphoreType.DMA((2, 2)),
                pltpu.SemaphoreType.DMA((2, GROUPS)),
                pltpu.SemaphoreType.DMA((2, heads)),
                pltpu.SemaphoreType.DMA((2,)),
                pltpu.SemaphoreType.DMA((2, GROUPS, reach)),
                pltpu.SemaphoreType.DMA((8,)),
            ],
            compiler_params=pltpu.CompilerParams(
                collective_id=0, has_side_effects=True, vmem_limit_bytes=56 << 20
            ),
        )(doc_lengths, queries, keys, values, out_grad)

    return jax.shard_map(
        local,
        mesh=mesh,
        in_specs=(P(("seq", "head"), None),) * 4 + (P(),),
        out_specs=(P(("seq", "head"), None),) * 4,
        check_vma=False,
    )
```

```python
import functools

import jax
import jax.numpy as jnp
from jax import lax
from jax.experimental import pallas as pl
from jax.experimental.pallas import tpu as pltpu
from jax.sharding import PartitionSpec as P

DH = 128
DOC_MOST = 16384
UNROLL = 4
GROUPS = 4
SCHEDULE = "L0T0L1T1P0L2T2P1L3T3P2P3A0A1A2A3M0M1U0U1M2Q0U2Q1U3M3Q2Q3F0F1F2F3"
KERNEL_VMEM_KIB = 60928
MESH = pl.DeviceIdType.MESH
F32 = jnp.float32
BF16 = jnp.bfloat16


def mm(a, b, ca, cb):
    return lax.dot_general(a, b, (((ca,), (cb,)), ((), ())), preferred_element_type=F32)


def feature(x):
    return jnp.where(x > 0, x + 1.0, jnp.exp(jnp.minimum(x, 0.0)))


def slope(x):
    return jnp.where(x > 0, 1.0, jnp.exp(jnp.minimum(x, 0.0)))


def kernel(
    cfg,
    len_ref,
    q_hbm,
    k_hbm,
    v_hbm,
    g_hbm,
    o_ref,
    gq_ref,
    gk_ref,
    gv_ref,
    q_ref,
    k_ref,
    v_ref,
    g_ref,
    fq_ref,
    fk_ref,
    sc_ref,
    ga_ref,
    att_ref,
    gfk_ref,
    gfv_ref,
    state_out,
    state_in,
    prefix_out,
    prefix_in,
    total_out,
    total_in,
    visible_ref,
    rows_ref,
    weight_ref,
    send_sem,
    state_sem,
    prefix_sem,
    zsend_sem,
    zrecv_sem,
    load_sem,
):
    heads, plane_seq, head_axis, planes, reach = cfg
    per_group = heads // GROUPS
    laps = per_group // UNROLL
    slab = DH // GROUPS
    seq = lax.axis_index("seq")
    place = lax.axis_index("head")
    z = seq // plane_seq
    mine = (seq % plane_seq) * head_axis + place
    block = z * heads + mine

    def peer(p):
        return (z * plane_seq + p // head_axis, p % head_axis)

    def plane_peer(other):
        return (other * plane_seq + seq % plane_seq, place)

    def cols(h):
        return pl.ds(pl.multiple_of(h * DH, DH), DH)

    loads = [
        pltpu.make_async_copy(src, dst, load_sem.at[n])
        for n, (src, dst) in enumerate(
            ((k_hbm, k_ref), (v_hbm, v_ref), (q_hbm, q_ref), (g_hbm, g_ref))
        )
    ]
    for load in loads:
        load.start()

    barrier = pltpu.get_barrier_semaphore()

    def greet(n, carry):
        pl.semaphore_signal(
            barrier, inc=1, device_id=peer((mine + n) % heads), device_id_type=MESH
        )
        return carry

    lax.fori_loop(1, heads, greet, 0)
    for n in range(1, planes):
        pl.semaphore_signal(
            barrier, inc=1, device_id=plane_peer((z + n) % planes), device_id_type=MESH
        )

    ends = []
    end = jnp.int32(0)
    for n in range(len_ref.shape[0]):
        end = end + len_ref[n]
        ends.append(end)

    def doc_of(where):
        return sum([(where >= e).astype(jnp.int32) for e in ends])

    def equal(a, b):
        return jnp.where(a == b, 1.0, 0.0).astype(F32)

    start = block * DH
    row_doc = doc_of(start + lax.broadcasted_iota(jnp.int32, (DH, DH), 0))
    col_doc = doc_of(start + lax.broadcasted_iota(jnp.int32, (DH, DH), 1))
    causal = lax.broadcasted_iota(jnp.int32, (DH, DH), 0) >= lax.broadcasted_iota(
        jnp.int32, (DH, DH), 1
    )
    visible_ref[...] = jnp.where(causal & (row_doc == col_doc), 1.0, 0.0).astype(F32)
    rows_ref[0] = jnp.where(row_doc == doc_of(start), 1.0, 0.0).astype(F32)
    rows_ref[1] = jnp.where(row_doc == doc_of(start + DH - 1), 1.0, 0.0).astype(F32)

    plane_start = z * (heads * DH)
    plane_first = doc_of(plane_start)
    plane_last = doc_of(plane_start + heads * DH - 1)

    def weigh(i, carry):
        begin = plane_start + i * DH
        before, first = doc_of(begin - 1), doc_of(begin)
        last, after = doc_of(begin + DH - 1), doc_of(begin + DH)
        weight_ref[0, i] = equal(last, plane_last)
        weight_ref[1, i] = equal(last, before)
        weight_ref[2, i] = equal(first, before)
        weight_ref[3, i] = equal(first, plane_first)
        weight_ref[4, i] = equal(first, after)
        weight_ref[5, i] = equal(last, after)
        return carry

    lax.fori_loop(0, heads, weigh, 0)

    def owned(g):
        return g * per_group + mine // GROUPS

    def slab_rows(s):
        return pl.ds(pl.multiple_of(s * slab, slab), slab)

    def state_copy(way, g, p):
        source = state_out.at[way, g * per_group + p // GROUPS, slab_rows(p % GROUPS)]
        return source, state_in.at[way, g, mine], state_sem.at[way, g]

    def prefix_copy(way, g, p):
        target = prefix_in.at[way, owned(g), slab_rows(mine % GROUPS)]
        return prefix_out.at[way, g, p], target, prefix_sem.at[way, owned(g)]

    def remote(refs, sem, p):
        return pltpu.make_async_remote_copy(
            src_ref=refs[0],
            dst_ref=refs[1],
            send_sem=sem,
            recv_sem=refs[2],
            device_id=peer(p),
            device_id_type=MESH,
        )

    def dispatch(refs, sem, p):
        own = p == mine

        @pl.when(own)
        def _():
            pltpu.make_async_copy(*refs).start()

        @pl.when(jnp.logical_not(own))
        def _():
            remote(refs, sem, p).start()

    def send_states(way, g, a):
        for s in range(GROUPS):
            p = a * GROUPS + (mine + s) % GROUPS
            dispatch(state_copy(way, g, p), send_sem.at[way, 0], p)

    def ahead(it, j):
        g, lap = it // laps, it % laps
        return g, (mine // GROUPS + lap * UNROLL + j) % per_group

    def forward_lap(it, carry):
        @pl.when(it < GROUPS * laps)
        def _():
            for j in range(UNROLL):
                g, a = ahead(it, j)
                h = g * per_group + a
                fk = feature(k_ref[:, cols(h)].astype(F32))
                fk_ref[h] = fk.astype(BF16)
                masked = (fk * rows_ref[1]).astype(BF16)
                state_out[0, h] = mm(masked, v_ref[:, cols(h)], 0, 0).astype(BF16)

        @pl.when(it == 1)
        def _():
            pl.semaphore_wait(barrier, heads - 1 + planes - 1)

        @pl.when(it > 0)
        def _():
            for j in range(UNROLL):
                g, a = ahead(it - 1, j)
                send_states(0, g, a)

        return carry

    def local_forward(g):
        def lap(it, carry):
            for j in range(UNROLL):
                h = g * per_group + it * UNROLL + j
                fq = feature(q_ref[:, cols(h)].astype(F32)).astype(BF16)
                fq_ref[h] = fq
                scores = (mm(fq, fk_ref[h], 1, 1) * visible_ref[...]).astype(BF16)
                sc_ref[h] = scores
                att_ref[h] = mm(scores, v_ref[:, cols(h)], 1, 0)
            return carry

        lax.fori_loop(0, laps, lap, 0)

    def total_copy(way, g, n):
        target = (z + n) % planes if way == 0 else (z + planes - n) % planes
        return pltpu.make_async_remote_copy(
            src_ref=total_out.at[way, g],
            dst_ref=total_in.at[way, g, n - 1],
            send_sem=zsend_sem.at[way],
            recv_sem=zrecv_sem.at[way, g, n - 1],
            device_id=plane_peer(target),
            device_id_type=MESH,
        )

    def sum_up(way, g):
        pltpu.make_async_copy(state_in.at[way, g], state_in.at[way, g], state_sem.at[way, g]).wait()

        def add(n, total):
            for j in range(4):
                i = n * 4 + j
                total = total + state_in[way, g, i].astype(F32) * weight_ref[3 * way, i]
            return total

        total = lax.fori_loop(0, heads // 4, add, jnp.zeros((slab, DH), F32))
        total_out[way, g] = total.astype(BF16)
        for n in range(1, reach + 1):
            total_copy(way, g, n).start()

    def scan(way, g):
        run = jnp.zeros((slab, DH), F32)
        for n in range(1, reach + 1):
            total_copy(way, g, n).wait_recv()
            if way == 0:
                source = z - n
                inside = source >= 0
                doc = doc_of((source + 1) * (heads * DH) - 1)
                near = doc_of(plane_start - 1)
            else:
                source = z + n
                inside = source < planes
                doc = doc_of(source * (heads * DH))
                near = doc_of(plane_start + heads * DH)
            scale = jnp.where(inside, equal(doc, near), 0.0)
            run = run + total_in[way, g, n - 1].astype(F32) * scale

        def step(n, run):
            for j in range(4):
                i = n * 4 + j
                i = i if way == 0 else heads - 1 - i
                prefix_out[way, g, i] = (run * weight_ref[3 * way + 2, i]).astype(BF16)
                run = state_in[way, g, i].astype(F32) + run * weight_ref[3 * way + 1, i]
            return run

        lax.fori_loop(0, heads // 4, step, run)

        def spread(n, carry):
            p = (mine + n) % heads
            dispatch(prefix_copy(way, g, p), send_sem.at[way, 1], p)
            return carry

        lax.fori_loop(0, heads, spread, 0)

    def arrive(way, h):
        pltpu.make_async_copy(prefix_in.at[way, h], prefix_in.at[way, h], prefix_sem.at[way, h]).wait()

    def behind(lap, j):
        return (mine // GROUPS + per_group - lap * UNROLL - j) % per_group

    def attend_lap(g, it, carry):
        @pl.when(it < laps)
        def _():
            spots = [behind(it, j) for j in range(UNROLL)]
            for a in spots:
                arrive(0, g * per_group + a)
            for a in spots:
                h = g * per_group + a
                head_rows = rows_ref[0]
                fq = fq_ref[h]
                att = att_ref[h] + mm(fq, prefix_in[0, h], 1, 0) * head_rows
                inv = lax.rsqrt(jnp.mean(att * att, axis=-1, keepdims=True) + 1e-05)
                normed = att * inv
                o_ref[:, cols(h)] = normed.astype(BF16)
                grad = g_ref[:, cols(h)].astype(F32)
                mean = jnp.mean(grad * normed, axis=-1, keepdims=True)
                ga = ((grad - normed * mean) * inv).astype(BF16)
                ga_ref[h] = ga
                masked = (fq.astype(F32) * head_rows).astype(BF16)
                state_out[1, h] = mm(masked, ga, 0, 0).astype(BF16)

        @pl.when(it > 0)
        def _():
            for j in range(UNROLL):
                send_states(1, g, behind(it - 1, j))

        return carry

    def local_back(g):
        def lap(it, carry):
            for j in range(UNROLL):
                h = g * per_group + it * UNROLL + j
                ga, fq, fk = ga_ref[h], fq_ref[h], fk_ref[h]
                grads = (mm(ga, v_ref[:, cols(h)], 1, 1) * visible_ref[...]).astype(BF16)
                gfq = mm(grads, fk, 1, 0) + mm(ga, prefix_in[0, h], 1, 1) * rows_ref[0]
                gq_ref[:, cols(h)] = (gfq * slope(q_ref[:, cols(h)].astype(F32))).astype(BF16)
                gfk_ref[h] = mm(grads, fq, 0, 0)
                gfv_ref[h] = mm(sc_ref[h], ga, 0, 0)
            return carry

        lax.fori_loop(0, laps, lap, 0)

    def finish_lap(g, it, carry):
        spots = [behind(it, j) for j in range(UNROLL)]
        for a in spots:
            arrive(1, g * per_group + a)
        for a in spots:
            h = g * per_group + a
            outgoing = prefix_in[1, h]
            gfk = gfk_ref[h] + mm(v_ref[:, cols(h)], outgoing, 1, 1) * rows_ref[1]
            gk_ref[:, cols(h)] = (gfk * slope(k_ref[:, cols(h)].astype(F32))).astype(BF16)
            gfv = gfv_ref[h] + mm(fk_ref[h], outgoing, 1, 0) * rows_ref[1]
            gv_ref[:, cols(h)] = gfv.astype(BF16)
        return carry

    def attend(g):
        lax.fori_loop(0, laps + 1, functools.partial(attend_lap, g), 0)

    def finish(g):
        lax.fori_loop(0, laps, functools.partial(finish_lap, g), 0)

    loads[0].wait()
    loads[1].wait()
    lax.fori_loop(0, GROUPS * laps + 1, forward_lap, 0)
    loads[2].wait()
    loads[3].wait()
    steps = {
        "L": local_forward,
        "T": functools.partial(sum_up, 0),
        "P": functools.partial(scan, 0),
        "A": attend,
        "M": local_back,
        "U": functools.partial(sum_up, 1),
        "Q": functools.partial(scan, 1),
        "F": finish,
    }
    for n in range(0, len(SCHEDULE), 2):
        steps[SCHEDULE[n]](int(SCHEDULE[n + 1]))
    for way in range(2):
        for n in range(2):
            sent = state_out.at[way, pl.ds(0, heads - 1)]
            pltpu.make_async_copy(sent, sent, send_sem.at[way, n]).wait()
        for n in range(1, reach + 1):
            pltpu.make_async_copy(total_out.at[way], total_out.at[way], zsend_sem.at[way]).wait()


def write_out(*refs):
    sources, targets, sem = refs[:4], refs[4:8], refs[8]
    copies = [pltpu.make_async_copy(sources[n], targets[n], sem.at[n]) for n in range(4)]
    for copy in copies:
        copy.start()
    for copy in copies:
        copy.wait()


def solution(mesh):
    seq_axis, head_axis = mesh.shape["seq"], mesh.shape["head"]

    def local(queries, keys, values, out_grad, doc_lengths):
        rows, width = queries.shape
        heads = width // DH
        plane_seq = heads // head_axis
        planes = seq_axis // plane_seq
        reach = min(planes - 1, -(-DOC_MOST // (heads * DH)))
        cfg = (heads, plane_seq, head_axis, planes, reach)
        flat = [pltpu.VMEM((rows, width), BF16)] * 4
        per_head = [pltpu.VMEM((heads, DH, DH), BF16)] * 4
        wide = [pltpu.VMEM((heads, DH, DH), F32)] * 3
        out = jax.ShapeDtypeStruct((rows, width), BF16)
        hbm = pl.BlockSpec(memory_space=pl.ANY)
        parts = pl.pallas_call(
            functools.partial(kernel, cfg),
            out_shape=(pltpu.VMEM((rows, width), BF16),) * 4,
            in_specs=[pl.BlockSpec(memory_space=pltpu.SMEM)] + [hbm] * 4,
            out_specs=(pl.BlockSpec(memory_space=pltpu.VMEM),) * 4,
            scratch_shapes=flat
            + per_head
            + wide
            + [
                pltpu.VMEM((2, heads, DH, DH), BF16),
                pltpu.VMEM((2, GROUPS, heads, DH // GROUPS, DH), BF16),
                pltpu.VMEM((2, GROUPS, heads, DH // GROUPS, DH), BF16),
                pltpu.VMEM((2, heads, DH, DH), BF16),
                pltpu.VMEM((2, GROUPS, DH // GROUPS, DH), BF16),
                pltpu.VMEM((2, GROUPS, reach, DH // GROUPS, DH), BF16),
                pltpu.VMEM((DH, DH), F32),
                pltpu.VMEM((2, DH, DH), F32),
                pltpu.SMEM((6, heads), F32),
                pltpu.SemaphoreType.DMA((2, 2)),
                pltpu.SemaphoreType.DMA((2, GROUPS)),
                pltpu.SemaphoreType.DMA((2, heads)),
                pltpu.SemaphoreType.DMA((2,)),
                pltpu.SemaphoreType.DMA((2, GROUPS, reach)),
                pltpu.SemaphoreType.DMA((4,)),
            ],
            compiler_params=pltpu.CompilerParams(
                collective_id=0, has_side_effects=True, vmem_limit_bytes=KERNEL_VMEM_KIB << 10
            ),
        )(doc_lengths, queries, keys, values, out_grad)
        return pl.pallas_call(
            write_out,
            out_shape=(out,) * 4,
            in_specs=[pl.BlockSpec(memory_space=pltpu.VMEM)] * 4,
            out_specs=(hbm,) * 4,
            scratch_shapes=[pltpu.SemaphoreType.DMA((4,))],
            compiler_params=pltpu.CompilerParams(vmem_limit_bytes=16 << 20),
        )(*parts)

    return jax.shard_map(
        local,
        mesh=mesh,
        in_specs=(P(("seq", "head"), None),) * 4 + (P(),),
        out_specs=(P(("seq", "head"), None),) * 4,
        check_vma=False,
    )
```

```python
import functools

import jax
import jax.numpy as jnp
from jax import lax
from jax.experimental import pallas as pl
from jax.experimental.pallas import tpu as pltpu
from jax.sharding import PartitionSpec as P

DH = 128
DOC_MOST = 16384
UNROLL = 8
GROUPS = 4
WRITES = 1
SPREAD = 32
SCHEDULE = "L0T0L1T1P0L2T2P1L3T3P2P3A0A1A2A3U0M0U1M1Q0U2M2Q1U3M3Q2Q3F0F1F2F3"
KERNEL_VMEM_KIB = 60928
MESH = pl.DeviceIdType.MESH
F32 = jnp.float32
BF16 = jnp.bfloat16


def mm(a, b, ca, cb):
    return lax.dot_general(a, b, (((ca,), (cb,)), ((), ())), preferred_element_type=F32)


def over(a, n):
    return lax.shift_right_logical(a, n.bit_length() - 1)


def modulo(a, n):
    return lax.bitwise_and(a, n - 1)


def feature(x):
    return jnp.where(x > 0, x + 1.0, jnp.exp(jnp.minimum(x, 0.0)))


def slope(x):
    return jnp.where(x > 0, 1.0, jnp.exp(jnp.minimum(x, 0.0)))


def kernel(
    cfg,
    len_ref,
    q_hbm,
    k_hbm,
    v_hbm,
    g_hbm,
    o_ref,
    gq_ref,
    gk_ref,
    gv_ref,
    q_ref,
    k_ref,
    v_ref,
    g_ref,
    fq_ref,
    fk_ref,
    sc_ref,
    ga_ref,
    att_ref,
    gfk_ref,
    gfv_ref,
    state_out,
    state_in,
    prefix_out,
    prefix_in,
    total_out,
    total_in,
    visible_ref,
    rows_ref,
    weight_ref,
    zweight_ref,
    send_sem,
    state_sem,
    prefix_sem,
    zsend_sem,
    zrecv_sem,
    load_sem,
):
    heads, plane_seq, head_axis, planes, reach = cfg
    per_group = heads // GROUPS
    laps = per_group // UNROLL
    slab = DH // GROUPS
    seq = lax.axis_index("seq")
    place = lax.axis_index("head")
    z = over(seq, plane_seq)
    mine = modulo(seq, plane_seq) * head_axis + place
    my_head, my_slab = over(mine, GROUPS), modulo(mine, GROUPS)
    block = z * heads + mine

    def peer(p):
        return (z * plane_seq + over(p, head_axis), modulo(p, head_axis))

    def plane_peer(other):
        return (other * plane_seq + modulo(seq, plane_seq), place)

    def cols(h):
        return pl.ds(pl.multiple_of(h * DH, DH), DH)

    part = per_group * DH
    first_loads = []
    for g in range(GROUPS):
        chunk = pl.ds(g * part, part)
        first_loads.append(
            [
                pltpu.make_async_copy(src.at[:, chunk], dst.at[:, chunk], load_sem.at[2 + 2 * g + n])
                for n, (src, dst) in enumerate(((k_hbm, k_ref), (v_hbm, v_ref)))
            ]
        )
    late_loads = [
        pltpu.make_async_copy(q_hbm, q_ref, load_sem.at[0]),
        pltpu.make_async_copy(g_hbm, g_ref, load_sem.at[1]),
    ]
    for pair in first_loads:
        for load in pair:
            load.start()

    barrier = pltpu.get_barrier_semaphore()

    def greet(n, carry):
        pl.semaphore_signal(
            barrier, inc=1, device_id=peer(modulo(mine + n, heads)), device_id_type=MESH
        )
        return carry

    lax.fori_loop(1, heads, greet, 0)
    for n in range(1, planes):
        pl.semaphore_signal(
            barrier, inc=1, device_id=plane_peer(modulo(z + n, planes)), device_id_type=MESH
        )

    ends = []
    end = jnp.int32(0)
    for n in range(len_ref.shape[0]):
        end = end + len_ref[n]
        ends.append(end)

    def doc_of(where):
        return sum([(where >= e).astype(jnp.int32) for e in ends])

    def equal(a, b):
        return jnp.where(a == b, 1.0, 0.0).astype(F32)

    start = block * DH
    row_doc = doc_of(start + lax.broadcasted_iota(jnp.int32, (DH, DH), 0))
    rows_ref[1] = jnp.where(row_doc == doc_of(start + DH - 1), 1.0, 0.0).astype(F32)

    def owned(g):
        return g * per_group + my_head

    def slab_rows(s):
        return pl.ds(pl.multiple_of(s * slab, slab), slab)

    def remote(refs, sem, p):
        return pltpu.make_async_remote_copy(
            src_ref=refs[0],
            dst_ref=refs[1],
            send_sem=sem,
            recv_sem=refs[2],
            device_id=peer(p),
            device_id_type=MESH,
        )

    def send_states(way, g, a, own):
        for n in range(GROUPS):
            s = modulo(mine + n, GROUPS)
            source = state_out.at[way, g * per_group + a, slab_rows(s)]
            refs = source, state_in.at[way, g, mine], state_sem.at[way, g]
            if own and n == 0:
                pltpu.make_async_copy(*refs).start()
            else:
                remote(refs, send_sem.at[way, 0], a * GROUPS + s).start()

    def ahead(lap, j):
        return modulo(my_head + lap * UNROLL + j, per_group)

    def forward_states(g, lap):
        for j in range(UNROLL):
            h = g * per_group + ahead(lap, j)
            fk = feature(k_ref[:, cols(h)].astype(F32))
            fk_ref[h] = fk.astype(BF16)
            masked = (fk * rows_ref[1]).astype(BF16)
            state_out[0, h] = mm(masked, v_ref[:, cols(h)], 0, 0).astype(BF16)

    def forward_sends(g, lap):
        for j in range(UNROLL):
            send_states(0, g, ahead(lap, j), lap == 0 and j == 0)

    def local_forward(g):
        def lap(it, carry):
            for j in range(UNROLL):
                h = g * per_group + it * UNROLL + j
                fq = feature(q_ref[:, cols(h)].astype(F32)).astype(BF16)
                fq_ref[h] = fq
                scores = (mm(fq, fk_ref[h], 1, 1) * visible_ref[...]).astype(BF16)
                sc_ref[h] = scores
                att_ref[h] = mm(scores, v_ref[:, cols(h)], 1, 0)
            return carry

        lax.fori_loop(0, laps, lap, 0)

    def total_copy(way, g, n):
        target = modulo(z + n if way == 0 else z + planes - n, planes)
        return pltpu.make_async_remote_copy(
            src_ref=total_out.at[way, g],
            dst_ref=total_in.at[way, g, n - 1],
            send_sem=zsend_sem.at[way],
            recv_sem=zrecv_sem.at[way, g, n - 1],
            device_id=plane_peer(target),
            device_id_type=MESH,
        )

    def sum_up(way, g):
        pltpu.make_async_copy(state_in.at[way, g], state_in.at[way, g], state_sem.at[way, g]).wait()

        def add(n, total):
            for j in range(4):
                i = n * 4 + j
                total = total + state_in[way, g, i].astype(F32) * weight_ref[3 * way, i]
            return total

        total = lax.fori_loop(0, heads // 4, add, jnp.zeros((slab, DH), F32))
        total_out[way, g] = total.astype(BF16)
        for n in range(1, reach + 1):
            total_copy(way, g, n).start()

    def scan(way, g):
        run = jnp.zeros((slab, DH), F32)
        for n in range(1, reach + 1):
            total_copy(way, g, n).wait_recv()
            scale = zweight_ref[way, n - 1]
            run = run + total_in[way, g, n - 1].astype(F32) * scale

        def step(n, run):
            for j in range(4):
                i = n * 4 + j
                i = i if way == 0 else heads - 1 - i
                prefix_out[way, g, i] = (run * weight_ref[3 * way + 2, i]).astype(BF16)
                run = state_in[way, g, i].astype(F32) + run * weight_ref[3 * way + 1, i]
            return run

        lax.fori_loop(0, heads // 4, step, run)

        def refs(p):
            target = prefix_in.at[way, owned(g), slab_rows(my_slab)]
            return prefix_out.at[way, g, p], target, prefix_sem.at[way, owned(g)]

        pltpu.make_async_copy(*refs(mine)).start()
        for n in range(1, SPREAD):
            p = modulo(mine + n, heads)
            remote(refs(p), send_sem.at[way, 1], p).start()

        def spread(n, carry):
            for j in range(SPREAD):
                p = modulo(mine + n * SPREAD + j, heads)
                remote(refs(p), send_sem.at[way, 1], p).start()
            return carry

        lax.fori_loop(1, heads // SPREAD, spread, 0)

    def arrive(way, h):
        pltpu.make_async_copy(prefix_in.at[way, h], prefix_in.at[way, h], prefix_sem.at[way, h]).wait()

    def behind(lap, j):
        return modulo(my_head + per_group - lap * UNROLL - j, per_group)

    def attend_states(g, lap):
        spots = [behind(lap, j) for j in range(UNROLL)]
        for a in spots:
            arrive(0, g * per_group + a)
        for a in spots:
            h = g * per_group + a
            head_rows = rows_ref[0]
            fq = fq_ref[h]
            att = att_ref[h] + mm(fq, prefix_in[0, h], 1, 0) * head_rows
            inv = lax.rsqrt(jnp.mean(att * att, axis=-1, keepdims=True) + 1e-05)
            normed = att * inv
            o_ref[:, cols(h)] = normed.astype(BF16)
            grad = g_ref[:, cols(h)].astype(F32)
            mean = jnp.mean(grad * normed, axis=-1, keepdims=True)
            ga = ((grad - normed * mean) * inv).astype(BF16)
            ga_ref[h] = ga
            masked = (fq.astype(F32) * head_rows).astype(BF16)
            state_out[1, h] = mm(masked, ga, 0, 0).astype(BF16)

    def attend_sends(g, lap):
        for j in range(UNROLL):
            send_states(1, g, behind(lap, j), lap == 0 and j == 0)

    def local_back(g):
        def lap(it, carry):
            for j in range(UNROLL):
                h = g * per_group + it * UNROLL + j
                ga, fq, fk = ga_ref[h], fq_ref[h], fk_ref[h]
                grads = (mm(ga, v_ref[:, cols(h)], 1, 1) * visible_ref[...]).astype(BF16)
                gfq = mm(grads, fk, 1, 0) + mm(ga, prefix_in[0, h], 1, 1) * rows_ref[0]
                gq_ref[:, cols(h)] = (gfq * slope(q_ref[:, cols(h)].astype(F32))).astype(BF16)
                gfk_ref[h] = mm(grads, fq, 0, 0)
                gfv_ref[h] = mm(sc_ref[h], ga, 0, 0)
            return carry

        lax.fori_loop(0, laps, lap, 0)

    def finish_lap(g, it, carry):
        spots = [behind(it, j) for j in range(UNROLL)]
        for a in spots:
            arrive(1, g * per_group + a)
        for a in spots:
            h = g * per_group + a
            outgoing = prefix_in[1, h]
            gfk = gfk_ref[h] + mm(v_ref[:, cols(h)], outgoing, 1, 1) * rows_ref[1]
            gk_ref[:, cols(h)] = (gfk * slope(k_ref[:, cols(h)].astype(F32))).astype(BF16)
            gfv = gfv_ref[h] + mm(fk_ref[h], outgoing, 1, 0) * rows_ref[1]
            gv_ref[:, cols(h)] = gfv.astype(BF16)
        return carry

    def attend(g):
        for lap in range(laps + 1):
            if lap < laps:
                attend_states(g, lap)
            if lap > 0:
                attend_sends(g, lap - 1)

    def finish(g):
        lax.fori_loop(0, laps, functools.partial(finish_lap, g), 0)

    order = [(g, lap) for g in range(GROUPS) for lap in range(laps)]
    for n in range(len(order) + 1):
        if n < len(order):
            if order[n][1] == 0:
                for load in first_loads[order[n][0]]:
                    load.wait()
            forward_states(*order[n])
        if n == 1:
            pl.semaphore_wait(barrier, heads - 1 + planes - 1)
        if n > 0:
            forward_sends(*order[n - 1])
    for load in late_loads:
        load.start()

    col_doc = doc_of(start + lax.broadcasted_iota(jnp.int32, (DH, DH), 1))
    causal = lax.broadcasted_iota(jnp.int32, (DH, DH), 0) >= lax.broadcasted_iota(
        jnp.int32, (DH, DH), 1
    )
    visible_ref[...] = jnp.where(causal & (row_doc == col_doc), 1.0, 0.0).astype(F32)
    rows_ref[0] = jnp.where(row_doc == doc_of(start), 1.0, 0.0).astype(F32)

    plane_start = z * (heads * DH)
    plane_first = doc_of(plane_start)
    plane_last = doc_of(plane_start + heads * DH - 1)

    def weigh(i, carry):
        begin = plane_start + i * DH
        before, first = doc_of(begin - 1), doc_of(begin)
        last, after = doc_of(begin + DH - 1), doc_of(begin + DH)
        weight_ref[0, i] = equal(last, plane_last)
        weight_ref[1, i] = equal(last, before)
        weight_ref[2, i] = equal(first, before)
        weight_ref[3, i] = equal(first, plane_first)
        weight_ref[4, i] = equal(first, after)
        weight_ref[5, i] = equal(last, after)
        return carry

    lax.fori_loop(0, heads, weigh, 0)
    before_plane, after_plane = doc_of(plane_start - 1), doc_of(plane_start + heads * DH)
    for n in range(1, reach + 1):
        lower = equal(doc_of((z - n + 1) * (heads * DH) - 1), before_plane)
        upper = equal(doc_of((z + n) * (heads * DH)), after_plane)
        zweight_ref[0, n - 1] = jnp.where(z >= n, lower, 0.0)
        zweight_ref[1, n - 1] = jnp.where(z + n < planes, upper, 0.0)

    for load in late_loads:
        load.wait()
    steps = {
        "L": local_forward,
        "T": functools.partial(sum_up, 0),
        "P": functools.partial(scan, 0),
        "A": attend,
        "M": local_back,
        "U": functools.partial(sum_up, 1),
        "Q": functools.partial(scan, 1),
        "F": finish,
    }
    for n in range(0, len(SCHEDULE), 2):
        steps[SCHEDULE[n]](int(SCHEDULE[n + 1]))
    for way in range(2):
        for n in range(2):
            sent = state_out.at[way, pl.ds(0, heads - 1)]
            pltpu.make_async_copy(sent, sent, send_sem.at[way, n]).wait()
        for n in range(1, reach + 1):
            pltpu.make_async_copy(total_out.at[way], total_out.at[way], zsend_sem.at[way]).wait()


def write_out(*refs):
    sources, targets, sem = refs[:4], refs[4:8], refs[8]
    step = sources[0].shape[0] // WRITES
    copies = [
        pltpu.make_async_copy(
            sources[n].at[pl.ds(m * step, step)], targets[n].at[pl.ds(m * step, step)], sem.at[n, m]
        )
        for n in range(4)
        for m in range(WRITES)
    ]
    for copy in copies:
        copy.start()
    for copy in copies:
        copy.wait()


def solution(mesh):
    seq_axis, head_axis = mesh.shape["seq"], mesh.shape["head"]

    def local(queries, keys, values, out_grad, doc_lengths):
        rows, width = queries.shape
        heads = width // DH
        plane_seq = heads // head_axis
        planes = seq_axis // plane_seq
        reach = min(planes - 1, -(-DOC_MOST // (heads * DH)))
        cfg = (heads, plane_seq, head_axis, planes, reach)
        flat = [pltpu.VMEM((rows, width), BF16)] * 4
        per_head = [pltpu.VMEM((heads, DH, DH), BF16)] * 4
        wide = [pltpu.VMEM((heads, DH, DH), F32)] * 3
        out = jax.ShapeDtypeStruct((rows, width), BF16)
        hbm = pl.BlockSpec(memory_space=pl.ANY)
        parts = pl.pallas_call(
            functools.partial(kernel, cfg),
            out_shape=(pltpu.VMEM((rows, width), BF16),) * 4,
            in_specs=[pl.BlockSpec(memory_space=pltpu.SMEM)] + [hbm] * 4,
            out_specs=(pl.BlockSpec(memory_space=pltpu.VMEM),) * 4,
            scratch_shapes=flat
            + per_head
            + wide
            + [
                pltpu.VMEM((2, heads, DH, DH), BF16),
                pltpu.VMEM((2, GROUPS, heads, DH // GROUPS, DH), BF16),
                pltpu.VMEM((2, GROUPS, heads, DH // GROUPS, DH), BF16),
                pltpu.VMEM((2, heads, DH, DH), BF16),
                pltpu.VMEM((2, GROUPS, DH // GROUPS, DH), BF16),
                pltpu.VMEM((2, GROUPS, reach, DH // GROUPS, DH), BF16),
                pltpu.VMEM((DH, DH), F32),
                pltpu.VMEM((2, DH, DH), F32),
                pltpu.SMEM((6, heads), F32),
                pltpu.SMEM((2, reach), F32),
                pltpu.SemaphoreType.DMA((2, 2)),
                pltpu.SemaphoreType.DMA((2, GROUPS)),
                pltpu.SemaphoreType.DMA((2, heads)),
                pltpu.SemaphoreType.DMA((2,)),
                pltpu.SemaphoreType.DMA((2, GROUPS, reach)),
                pltpu.SemaphoreType.DMA((2 + 2 * GROUPS,)),
            ],
            compiler_params=pltpu.CompilerParams(
                collective_id=0, has_side_effects=True, vmem_limit_bytes=KERNEL_VMEM_KIB << 10
            ),
        )(doc_lengths, queries, keys, values, out_grad)
        return pl.pallas_call(
            write_out,
            out_shape=(out,) * 4,
            in_specs=[pl.BlockSpec(memory_space=pltpu.VMEM)] * 4,
            out_specs=(hbm,) * 4,
            scratch_shapes=[pltpu.SemaphoreType.DMA((4, WRITES))],
            compiler_params=pltpu.CompilerParams(vmem_limit_bytes=16 << 20),
        )(*parts)

    return jax.shard_map(
        local,
        mesh=mesh,
        in_specs=(P(("seq", "head"), None),) * 4 + (P(),),
        out_specs=(P(("seq", "head"), None),) * 4,
        check_vma=False,
    )
```

```python
import functools

import jax
import jax.numpy as jnp
from jax import lax
from jax.experimental import pallas as pl
from jax.experimental.pallas import tpu as pltpu
from jax.sharding import PartitionSpec as P

DH = 128
DOC_MOST = 16384
UNROLL = 8
GROUPS = 4
WRITES = 1
SPREAD = 32
SCHEDULE = "L0T0L1T1P0L2T2P1L3T3P2P3A0A1A2A3U0M0U1M1Q0U2M2Q1U3M3Q2Q3F0F1F2F3"
KERNEL_VMEM_KIB = 60928
MESH = pl.DeviceIdType.MESH
F32 = jnp.float32
BF16 = jnp.bfloat16


def mm(a, b, ca, cb):
    return lax.dot_general(a, b, (((ca,), (cb,)), ((), ())), preferred_element_type=F32)


def over(a, n):
    return lax.shift_right_logical(a, n.bit_length() - 1)


def modulo(a, n):
    return lax.bitwise_and(a, n - 1)


def feature(x):
    return jnp.where(x > 0, x + 1.0, jnp.exp(jnp.minimum(x, 0.0)))


def slope(x):
    return jnp.where(x > 0, 1.0, jnp.exp(jnp.minimum(x, 0.0)))


def kernel(
    cfg,
    len_ref,
    q_hbm,
    k_hbm,
    v_hbm,
    g_hbm,
    o_ref,
    gq_ref,
    gk_ref,
    gv_ref,
    q_ref,
    k_ref,
    v_ref,
    g_ref,
    fq_ref,
    fqm_ref,
    fk_ref,
    sc_ref,
    ga_ref,
    att_ref,
    gfk_ref,
    gfv_ref,
    state_out,
    state_in,
    prefix_out,
    prefix_in,
    total_out,
    total_in,
    visible_ref,
    rows_ref,
    weight_ref,
    zweight_ref,
    send_sem,
    state_sem,
    prefix_sem,
    zsend_sem,
    zrecv_sem,
    load_sem,
):
    heads, plane_seq, head_axis, planes, reach = cfg
    per_group = heads // GROUPS
    laps = per_group // UNROLL
    slab = DH // GROUPS
    seq = lax.axis_index("seq")
    place = lax.axis_index("head")
    z = over(seq, plane_seq)
    mine = modulo(seq, plane_seq) * head_axis + place
    my_head, my_slab = over(mine, GROUPS), modulo(mine, GROUPS)
    block = z * heads + mine

    def peer(p):
        return (z * plane_seq + over(p, head_axis), modulo(p, head_axis))

    def plane_peer(other):
        return (other * plane_seq + modulo(seq, plane_seq), place)

    def cols(h):
        return pl.ds(pl.multiple_of(h * DH, DH), DH)

    part = per_group * DH
    first_loads = []
    for g in range(GROUPS):
        chunk = pl.ds(g * part, part)
        first_loads.append(
            [
                pltpu.make_async_copy(src.at[:, chunk], dst.at[:, chunk], load_sem.at[2 + 2 * g + n])
                for n, (src, dst) in enumerate(((k_hbm, k_ref), (v_hbm, v_ref)))
            ]
        )
    late_loads = [
        pltpu.make_async_copy(q_hbm, q_ref, load_sem.at[0]),
        pltpu.make_async_copy(g_hbm, g_ref, load_sem.at[1]),
    ]
    for pair in first_loads:
        for load in pair:
            load.start()

    barrier = pltpu.get_barrier_semaphore()

    def greet(n, carry):
        pl.semaphore_signal(
            barrier, inc=1, device_id=peer(modulo(mine + n, heads)), device_id_type=MESH
        )
        return carry

    lax.fori_loop(1, heads, greet, 0)
    for n in range(1, planes):
        pl.semaphore_signal(
            barrier, inc=1, device_id=plane_peer(modulo(z + n, planes)), device_id_type=MESH
        )

    ends = []
    end = jnp.int32(0)
    for n in range(len_ref.shape[0]):
        end = end + len_ref[n]
        ends.append(end)

    def doc_of(where):
        return sum([(where >= e).astype(jnp.int32) for e in ends])

    def equal(a, b):
        return jnp.where(a == b, 1.0, 0.0).astype(F32)

    start = block * DH
    row_doc = doc_of(start + lax.broadcasted_iota(jnp.int32, (DH, DH), 0))
    rows_ref[1] = jnp.where(row_doc == doc_of(start + DH - 1), 1.0, 0.0).astype(F32)

    def owned(g):
        return g * per_group + my_head

    def slab_rows(s):
        return pl.ds(pl.multiple_of(s * slab, slab), slab)

    def remote(refs, sem, p):
        return pltpu.make_async_remote_copy(
            src_ref=refs[0],
            dst_ref=refs[1],
            send_sem=sem,
            recv_sem=refs[2],
            device_id=peer(p),
            device_id_type=MESH,
        )

    def send_states(way, g, a, own):
        for n in range(GROUPS):
            s = modulo(mine + n, GROUPS)
            source = state_out.at[way, g * per_group + a, slab_rows(s)]
            refs = source, state_in.at[way, g, mine], state_sem.at[way, g]
            if own and n == 0:
                pltpu.make_async_copy(*refs).start()
            else:
                remote(refs, send_sem.at[way, 0], a * GROUPS + s).start()

    def ahead(lap, j):
        return modulo(my_head + lap * UNROLL + j, per_group)

    def forward_states(g, lap):
        for j in range(UNROLL):
            h = g * per_group + ahead(lap, j)
            fk = feature(k_ref[:, cols(h)].astype(F32))
            fk_ref[h] = fk.astype(BF16)
            masked = (fk * rows_ref[1]).astype(BF16)
            state_out[0, h] = mm(masked, v_ref[:, cols(h)], 0, 0).astype(BF16)

    def forward_sends(g, lap):
        for j in range(UNROLL):
            send_states(0, g, ahead(lap, j), lap == 0 and j == 0)

    def local_forward(g):
        def lap(it, carry):
            for j in range(UNROLL):
                h = g * per_group + it * UNROLL + j
                wide = feature(q_ref[:, cols(h)].astype(F32))
                fq = wide.astype(BF16)
                fq_ref[h] = fq
                fqm_ref[h] = (wide * rows_ref[0]).astype(BF16)
                scores = (mm(fq, fk_ref[h], 1, 1) * visible_ref[...]).astype(BF16)
                sc_ref[h] = scores
                att_ref[h] = mm(scores, v_ref[:, cols(h)], 1, 0)
            return carry

        lax.fori_loop(0, laps, lap, 0)

    def total_copy(way, g, n):
        target = modulo(z + n if way == 0 else z + planes - n, planes)
        return pltpu.make_async_remote_copy(
            src_ref=total_out.at[way, g],
            dst_ref=total_in.at[way, g, n - 1],
            send_sem=zsend_sem.at[way],
            recv_sem=zrecv_sem.at[way, g, n - 1],
            device_id=plane_peer(target),
            device_id_type=MESH,
        )

    def sum_up(way, g):
        pltpu.make_async_copy(state_in.at[way, g], state_in.at[way, g], state_sem.at[way, g]).wait()

        def add(n, total):
            for j in range(4):
                i = n * 4 + j
                total = total + state_in[way, g, i].astype(F32) * weight_ref[3 * way, i]
            return total

        total = lax.fori_loop(0, heads // 4, add, jnp.zeros((slab, DH), F32))
        total_out[way, g] = total.astype(BF16)
        for n in range(reach, 0, -1):
            total_copy(way, g, n).start()

    def scan(way, g):
        run = jnp.zeros((slab, DH), F32)
        for n in range(1, reach + 1):
            total_copy(way, g, n).wait_recv()
            scale = zweight_ref[way, n - 1]
            run = run + total_in[way, g, n - 1].astype(F32) * scale

        def step(n, run):
            for j in range(4):
                i = n * 4 + j
                i = i if way == 0 else heads - 1 - i
                prefix_out[way, g, i] = (run * weight_ref[3 * way + 2, i]).astype(BF16)
                run = state_in[way, g, i].astype(F32) + run * weight_ref[3 * way + 1, i]
            return run

        lax.fori_loop(0, heads // 4, step, run)

        def refs(p):
            target = prefix_in.at[way, owned(g), slab_rows(my_slab)]
            return prefix_out.at[way, g, p], target, prefix_sem.at[way, owned(g)]

        pltpu.make_async_copy(*refs(mine)).start()
        for n in range(1, SPREAD):
            p = modulo(mine + n, heads)
            remote(refs(p), send_sem.at[way, 1], p).start()

        def spread(n, carry):
            for j in range(SPREAD):
                p = modulo(mine + n * SPREAD + j, heads)
                remote(refs(p), send_sem.at[way, 1], p).start()
            return carry

        lax.fori_loop(1, heads // SPREAD, spread, 0)

    def arrive(way, h):
        pltpu.make_async_copy(prefix_in.at[way, h], prefix_in.at[way, h], prefix_sem.at[way, h]).wait()

    def behind(lap, j):
        return modulo(my_head + per_group - lap * UNROLL - j, per_group)

    def attend_states(g, lap):
        spots = [behind(lap, j) for j in range(UNROLL)]
        for a in spots:
            arrive(0, g * per_group + a)
        for a in spots:
            h = g * per_group + a
            masked = fqm_ref[h]
            att = att_ref[h] + mm(masked, prefix_in[0, h], 1, 0)
            inv = lax.rsqrt(jnp.mean(att * att, axis=-1, keepdims=True) + 1e-05)
            normed = att * inv
            o_ref[:, cols(h)] = normed.astype(BF16)
            grad = g_ref[:, cols(h)].astype(F32)
            mean = jnp.mean(grad * normed, axis=-1, keepdims=True)
            ga = ((grad - normed * mean) * inv).astype(BF16)
            ga_ref[h] = ga
            state_out[1, h] = mm(masked, ga, 0, 0).astype(BF16)

    def attend_sends(g, lap):
        for j in range(UNROLL):
            send_states(1, g, behind(lap, j), lap == 0 and j == 0)

    def local_back(g):
        def lap(it, carry):
            for j in range(UNROLL):
                h = g * per_group + it * UNROLL + j
                ga, fq, fk = ga_ref[h], fq_ref[h], fk_ref[h]
                grads = (mm(ga, v_ref[:, cols(h)], 1, 1) * visible_ref[...]).astype(BF16)
                gfq = mm(grads, fk, 1, 0) + mm(ga, prefix_in[0, h], 1, 1) * rows_ref[0]
                gq_ref[:, cols(h)] = (gfq * slope(q_ref[:, cols(h)].astype(F32))).astype(BF16)
                gfk_ref[h] = mm(grads, fq, 0, 0)
                gfv_ref[h] = mm(sc_ref[h], ga, 0, 0)
            return carry

        lax.fori_loop(0, laps, lap, 0)

    def finish_lap(g, it, carry):
        spots = [behind(it, j) for j in range(UNROLL)]
        for a in spots:
            arrive(1, g * per_group + a)
        for a in spots:
            h = g * per_group + a
            outgoing = prefix_in[1, h]
            gfk = gfk_ref[h] + mm(v_ref[:, cols(h)], outgoing, 1, 1) * rows_ref[1]
            gk_ref[:, cols(h)] = (gfk * slope(k_ref[:, cols(h)].astype(F32))).astype(BF16)
            gfv = gfv_ref[h] + mm(fk_ref[h], outgoing, 1, 0) * rows_ref[1]
            gv_ref[:, cols(h)] = gfv.astype(BF16)
        return carry

    def attend(g):
        for lap in range(laps + 1):
            if lap < laps:
                attend_states(g, lap)
            if lap > 0:
                attend_sends(g, lap - 1)

    def finish(g):
        lax.fori_loop(0, laps, functools.partial(finish_lap, g), 0)

    order = [(g, lap) for g in range(GROUPS) for lap in range(laps)]
    for n in range(len(order) + 1):
        if n < len(order):
            if order[n][1] == 0:
                for load in first_loads[order[n][0]]:
                    load.wait()
            forward_states(*order[n])
        if n == 1:
            pl.semaphore_wait(barrier, heads - 1 + planes - 1)
        if n > 0:
            forward_sends(*order[n - 1])
    for load in late_loads:
        load.start()

    col_doc = doc_of(start + lax.broadcasted_iota(jnp.int32, (DH, DH), 1))
    causal = lax.broadcasted_iota(jnp.int32, (DH, DH), 0) >= lax.broadcasted_iota(
        jnp.int32, (DH, DH), 1
    )
    visible_ref[...] = jnp.where(causal & (row_doc == col_doc), 1.0, 0.0).astype(F32)
    rows_ref[0] = jnp.where(row_doc == doc_of(start), 1.0, 0.0).astype(F32)

    plane_start = z * (heads * DH)
    plane_first = doc_of(plane_start)
    plane_last = doc_of(plane_start + heads * DH - 1)

    def weigh(i, carry):
        begin = plane_start + i * DH
        before, first = doc_of(begin - 1), doc_of(begin)
        last, after = doc_of(begin + DH - 1), doc_of(begin + DH)
        weight_ref[0, i] = equal(last, plane_last)
        weight_ref[1, i] = equal(last, before)
        weight_ref[2, i] = equal(first, before)
        weight_ref[3, i] = equal(first, plane_first)
        weight_ref[4, i] = equal(first, after)
        weight_ref[5, i] = equal(last, after)
        return carry

    lax.fori_loop(0, heads, weigh, 0)
    before_plane, after_plane = doc_of(plane_start - 1), doc_of(plane_start + heads * DH)
    for n in range(1, reach + 1):
        lower = equal(doc_of((z - n + 1) * (heads * DH) - 1), before_plane)
        upper = equal(doc_of((z + n) * (heads * DH)), after_plane)
        zweight_ref[0, n - 1] = jnp.where(z >= n, lower, 0.0)
        zweight_ref[1, n - 1] = jnp.where(z + n < planes, upper, 0.0)

    for load in late_loads:
        load.wait()
    steps = {
        "L": local_forward,
        "T": functools.partial(sum_up, 0),
        "P": functools.partial(scan, 0),
        "A": attend,
        "M": local_back,
        "U": functools.partial(sum_up, 1),
        "Q": functools.partial(scan, 1),
        "F": finish,
    }
    for n in range(0, len(SCHEDULE), 2):
        steps[SCHEDULE[n]](int(SCHEDULE[n + 1]))
    for way in range(2):
        for n in range(2):
            sent = state_out.at[way, pl.ds(0, heads - 1)]
            pltpu.make_async_copy(sent, sent, send_sem.at[way, n]).wait()
        for n in range(1, reach + 1):
            pltpu.make_async_copy(total_out.at[way], total_out.at[way], zsend_sem.at[way]).wait()


def write_out(*refs):
    sources, targets, sem = refs[:4], refs[4:8], refs[8]
    step = sources[0].shape[0] // WRITES
    copies = [
        pltpu.make_async_copy(
            sources[n].at[pl.ds(m * step, step)], targets[n].at[pl.ds(m * step, step)], sem.at[n, m]
        )
        for n in range(4)
        for m in range(WRITES)
    ]
    for copy in copies:
        copy.start()
    for copy in copies:
        copy.wait()


def solution(mesh):
    seq_axis, head_axis = mesh.shape["seq"], mesh.shape["head"]

    def local(queries, keys, values, out_grad, doc_lengths):
        rows, width = queries.shape
        heads = width // DH
        plane_seq = heads // head_axis
        planes = seq_axis // plane_seq
        reach = min(planes - 1, -(-DOC_MOST // (heads * DH)))
        cfg = (heads, plane_seq, head_axis, planes, reach)
        flat = [pltpu.VMEM((rows, width), BF16)] * 4
        per_head = [pltpu.VMEM((heads, DH, DH), BF16)] * 5
        wide = [pltpu.VMEM((heads, DH, DH), F32)] * 3
        out = jax.ShapeDtypeStruct((rows, width), BF16)
        hbm = pl.BlockSpec(memory_space=pl.ANY)
        parts = pl.pallas_call(
            functools.partial(kernel, cfg),
            out_shape=(pltpu.VMEM((rows, width), BF16),) * 4,
            in_specs=[pl.BlockSpec(memory_space=pltpu.SMEM)] + [hbm] * 4,
            out_specs=(pl.BlockSpec(memory_space=pltpu.VMEM),) * 4,
            scratch_shapes=flat
            + per_head
            + wide
            + [
                pltpu.VMEM((2, heads, DH, DH), BF16),
                pltpu.VMEM((2, GROUPS, heads, DH // GROUPS, DH), BF16),
                pltpu.VMEM((2, GROUPS, heads, DH // GROUPS, DH), BF16),
                pltpu.VMEM((2, heads, DH, DH), BF16),
                pltpu.VMEM((2, GROUPS, DH // GROUPS, DH), BF16),
                pltpu.VMEM((2, GROUPS, reach, DH // GROUPS, DH), BF16),
                pltpu.VMEM((DH, DH), F32),
                pltpu.VMEM((2, DH, DH), F32),
                pltpu.SMEM((6, heads), F32),
                pltpu.SMEM((2, reach), F32),
                pltpu.SemaphoreType.DMA((2, 2)),
                pltpu.SemaphoreType.DMA((2, GROUPS)),
                pltpu.SemaphoreType.DMA((2, heads)),
                pltpu.SemaphoreType.DMA((2,)),
                pltpu.SemaphoreType.DMA((2, GROUPS, reach)),
                pltpu.SemaphoreType.DMA((2 + 2 * GROUPS,)),
            ],
            compiler_params=pltpu.CompilerParams(
                collective_id=0, has_side_effects=True, vmem_limit_bytes=KERNEL_VMEM_KIB << 10
            ),
        )(doc_lengths, queries, keys, values, out_grad)
        return pl.pallas_call(
            write_out,
            out_shape=(out,) * 4,
            in_specs=[pl.BlockSpec(memory_space=pltpu.VMEM)] * 4,
            out_specs=(hbm,) * 4,
            scratch_shapes=[pltpu.SemaphoreType.DMA((4, WRITES))],
            compiler_params=pltpu.CompilerParams(vmem_limit_bytes=16 << 20),
        )(*parts)

    return jax.shard_map(
        local,
        mesh=mesh,
        in_specs=(P(("seq", "head"), None),) * 4 + (P(),),
        out_specs=(P(("seq", "head"), None),) * 4,
        check_vma=False,
    )
```

```python
import functools

import jax
import jax.numpy as jnp
from jax import lax
from jax.experimental import pallas as pl
from jax.experimental.pallas import tpu as pltpu
from jax.sharding import PartitionSpec as P

DH = 128
DOC_MOST = 16384
UNROLL = 8
GROUPS = 4
WRITES = 1
SPREAD = 32
SCHEDULE = "L0T0L1T1P0L2T2P1L3T3P2P3A0A1A2A3U0M0U1M1Q0U2M2Q1U3M3Q2Q3F0F1F2F3"
KERNEL_VMEM_KIB = 60928
MESH = pl.DeviceIdType.MESH
F32 = jnp.float32
BF16 = jnp.bfloat16


def mm(a, b, ca, cb):
    return lax.dot_general(a, b, (((ca,), (cb,)), ((), ())), preferred_element_type=F32)


def over(a, n):
    return lax.shift_right_logical(a, n.bit_length() - 1)


def modulo(a, n):
    return lax.bitwise_and(a, n - 1)


def feature(x):
    return jnp.where(x > 0, x + 1.0, jnp.exp(jnp.minimum(x, 0.0)))


def slope(x):
    return jnp.where(x > 0, 1.0, jnp.exp(jnp.minimum(x, 0.0)))


def kernel(
    cfg,
    len_ref,
    q_hbm,
    k_hbm,
    v_hbm,
    g_hbm,
    o_ref,
    gq_ref,
    gk_ref,
    gv_ref,
    q_ref,
    k_ref,
    v_ref,
    g_ref,
    fq_ref,
    fqm_ref,
    fk_ref,
    sc_ref,
    ga_ref,
    fkm_ref,
    vm_ref,
    slope_ref,
    att_ref,
    gfk_ref,
    gfv_ref,
    state_out,
    state_in,
    prefix_out,
    prefix_in,
    total_out,
    total_in,
    visible_ref,
    rows_ref,
    weight_ref,
    zweight_ref,
    send_sem,
    state_sem,
    prefix_sem,
    zsend_sem,
    zrecv_sem,
    load_sem,
):
    heads, plane_seq, head_axis, planes, reach = cfg
    per_group = heads // GROUPS
    laps = per_group // UNROLL
    slab = DH // GROUPS
    seq = lax.axis_index("seq")
    place = lax.axis_index("head")
    z = over(seq, plane_seq)
    mine = modulo(seq, plane_seq) * head_axis + place
    my_head, my_slab = over(mine, GROUPS), modulo(mine, GROUPS)
    block = z * heads + mine

    def peer(p):
        return (z * plane_seq + over(p, head_axis), modulo(p, head_axis))

    def plane_peer(other):
        return (other * plane_seq + modulo(seq, plane_seq), place)

    def cols(h):
        return pl.ds(pl.multiple_of(h * DH, DH), DH)

    part = per_group * DH
    first_loads = []
    for g in range(GROUPS):
        chunk = pl.ds(g * part, part)
        first_loads.append(
            [
                pltpu.make_async_copy(src.at[:, chunk], dst.at[:, chunk], load_sem.at[2 + 2 * g + n])
                for n, (src, dst) in enumerate(((k_hbm, k_ref), (v_hbm, v_ref)))
            ]
        )
    late_loads = [
        pltpu.make_async_copy(q_hbm, q_ref, load_sem.at[0]),
        pltpu.make_async_copy(g_hbm, g_ref, load_sem.at[1]),
    ]
    for pair in first_loads:
        for load in pair:
            load.start()

    barrier = pltpu.get_barrier_semaphore()

    def greet(n, carry):
        pl.semaphore_signal(
            barrier, inc=1, device_id=peer(modulo(mine + n, heads)), device_id_type=MESH
        )
        return carry

    lax.fori_loop(1, heads, greet, 0)
    for n in range(1, planes):
        pl.semaphore_signal(
            barrier, inc=1, device_id=plane_peer(modulo(z + n, planes)), device_id_type=MESH
        )

    ends = []
    end = jnp.int32(0)
    for n in range(len_ref.shape[0]):
        end = end + len_ref[n]
        ends.append(end)

    def doc_of(where):
        return sum([(where >= e).astype(jnp.int32) for e in ends])

    def equal(a, b):
        return jnp.where(a == b, 1.0, 0.0).astype(F32)

    start = block * DH
    row_doc = doc_of(start + lax.broadcasted_iota(jnp.int32, (DH, DH), 0))
    rows_ref[1] = jnp.where(row_doc == doc_of(start + DH - 1), 1.0, 0.0).astype(F32)

    def owned(g):
        return g * per_group + my_head

    def slab_rows(s):
        return pl.ds(pl.multiple_of(s * slab, slab), slab)

    def remote(refs, sem, p):
        return pltpu.make_async_remote_copy(
            src_ref=refs[0],
            dst_ref=refs[1],
            send_sem=sem,
            recv_sem=refs[2],
            device_id=peer(p),
            device_id_type=MESH,
        )

    def send_states(way, g, a, own):
        for n in range(GROUPS):
            s = modulo(mine + n, GROUPS)
            source = state_out.at[way, g * per_group + a, slab_rows(s)]
            refs = source, state_in.at[way, g, mine], state_sem.at[way, g]
            if own and n == 0:
                pltpu.make_async_copy(*refs).start()
            else:
                remote(refs, send_sem.at[way, 0], a * GROUPS + s).start()

    def ahead(lap, j):
        return modulo(my_head + lap * UNROLL + j, per_group)

    def forward_states(g, lap):
        for j in range(UNROLL):
            h = g * per_group + ahead(lap, j)
            fk = feature(k_ref[:, cols(h)].astype(F32))
            fk_ref[h] = fk.astype(BF16)
            masked = (fk * rows_ref[1]).astype(BF16)
            fkm_ref[h] = masked
            state_out[0, h] = mm(masked, v_ref[:, cols(h)], 0, 0).astype(BF16)

    def forward_sends(g, lap):
        for j in range(UNROLL):
            send_states(0, g, ahead(lap, j), lap == 0 and j == 0)

    def local_forward(g):
        def lap(it, carry):
            for j in range(UNROLL):
                h = g * per_group + it * UNROLL + j
                wide = feature(q_ref[:, cols(h)].astype(F32))
                fq = wide.astype(BF16)
                fq_ref[h] = fq
                fqm_ref[h] = (wide * rows_ref[0]).astype(BF16)
                vm_ref[h] = (v_ref[:, cols(h)].astype(F32) * rows_ref[1]).astype(BF16)
                slope_ref[h] = slope(k_ref[:, cols(h)].astype(F32))
                scores = (mm(fq, fk_ref[h], 1, 1) * visible_ref[...]).astype(BF16)
                sc_ref[h] = scores
                att_ref[h] = mm(scores, v_ref[:, cols(h)], 1, 0)
            return carry

        lax.fori_loop(0, laps, lap, 0)

    def total_copy(way, g, n):
        target = modulo(z + n if way == 0 else z + planes - n, planes)
        return pltpu.make_async_remote_copy(
            src_ref=total_out.at[way, g],
            dst_ref=total_in.at[way, g, n - 1],
            send_sem=zsend_sem.at[way],
            recv_sem=zrecv_sem.at[way, g, n - 1],
            device_id=plane_peer(target),
            device_id_type=MESH,
        )

    def sum_up(way, g):
        pltpu.make_async_copy(state_in.at[way, g], state_in.at[way, g], state_sem.at[way, g]).wait()

        def add(n, total):
            for j in range(4):
                i = n * 4 + j
                total = total + state_in[way, g, i].astype(F32) * weight_ref[3 * way, i]
            return total

        total = lax.fori_loop(0, heads // 4, add, jnp.zeros((slab, DH), F32))
        total_out[way, g] = total.astype(BF16)
        for n in range(reach, 0, -1):
            total_copy(way, g, n).start()

    def scan(way, g):
        run = jnp.zeros((slab, DH), F32)
        for n in range(1, reach + 1):
            total_copy(way, g, n).wait_recv()
            scale = zweight_ref[way, n - 1]
            run = run + total_in[way, g, n - 1].astype(F32) * scale

        def step(n, run):
            for j in range(4):
                i = n * 4 + j
                i = i if way == 0 else heads - 1 - i
                prefix_out[way, g, i] = (run * weight_ref[3 * way + 2, i]).astype(BF16)
                run = state_in[way, g, i].astype(F32) + run * weight_ref[3 * way + 1, i]
            return run

        lax.fori_loop(0, heads // 4, step, run)

        def refs(p):
            target = prefix_in.at[way, owned(g), slab_rows(my_slab)]
            return prefix_out.at[way, g, p], target, prefix_sem.at[way, owned(g)]

        pltpu.make_async_copy(*refs(mine)).start()
        for n in range(1, SPREAD):
            p = modulo(mine + n, heads)
            remote(refs(p), send_sem.at[way, 1], p).start()

        def spread(n, carry):
            for j in range(SPREAD):
                p = modulo(mine + n * SPREAD + j, heads)
                remote(refs(p), send_sem.at[way, 1], p).start()
            return carry

        lax.fori_loop(1, heads // SPREAD, spread, 0)

    def arrive(way, h):
        pltpu.make_async_copy(prefix_in.at[way, h], prefix_in.at[way, h], prefix_sem.at[way, h]).wait()

    def behind(lap, j):
        return modulo(my_head + per_group - lap * UNROLL - j, per_group)

    def attend_states(g, lap):
        spots = [behind(lap, j) for j in range(UNROLL)]
        for a in spots:
            arrive(0, g * per_group + a)
        for a in spots:
            h = g * per_group + a
            masked = fqm_ref[h]
            att = att_ref[h] + mm(masked, prefix_in[0, h], 1, 0)
            inv = lax.rsqrt(jnp.mean(att * att, axis=-1, keepdims=True) + 1e-05)
            normed = att * inv
            o_ref[:, cols(h)] = normed.astype(BF16)
            grad = g_ref[:, cols(h)].astype(F32)
            mean = jnp.mean(grad * normed, axis=-1, keepdims=True)
            ga = ((grad - normed * mean) * inv).astype(BF16)
            ga_ref[h] = ga
            state_out[1, h] = mm(masked, ga, 0, 0).astype(BF16)

    def attend_sends(g, lap):
        for j in range(UNROLL):
            send_states(1, g, behind(lap, j), lap == 0 and j == 0)

    def local_back(g):
        def lap(it, carry):
            for j in range(UNROLL):
                h = g * per_group + it * UNROLL + j
                ga, fq, fk = ga_ref[h], fq_ref[h], fk_ref[h]
                grads = (mm(ga, v_ref[:, cols(h)], 1, 1) * visible_ref[...]).astype(BF16)
                gfq = mm(grads, fk, 1, 0) + mm(ga, prefix_in[0, h], 1, 1) * rows_ref[0]
                gq_ref[:, cols(h)] = (gfq * slope(q_ref[:, cols(h)].astype(F32))).astype(BF16)
                gfk_ref[h] = mm(grads, fq, 0, 0)
                gfv_ref[h] = mm(sc_ref[h], ga, 0, 0)
            return carry

        lax.fori_loop(0, laps, lap, 0)

    def finish_lap(g, it, carry):
        spots = [behind(it, j) for j in range(UNROLL)]
        for a in spots:
            arrive(1, g * per_group + a)
        for a in spots:
            h = g * per_group + a
            outgoing = prefix_in[1, h]
            gfk = gfk_ref[h] + mm(vm_ref[h], outgoing, 1, 1)
            gk_ref[:, cols(h)] = (gfk * slope_ref[h]).astype(BF16)
            gfv = gfv_ref[h] + mm(fkm_ref[h], outgoing, 1, 0)
            gv_ref[:, cols(h)] = gfv.astype(BF16)
        return carry

    def attend(g):
        for lap in range(laps + 1):
            if lap < laps:
                attend_states(g, lap)
            if lap > 0:
                attend_sends(g, lap - 1)

    def finish(g):
        lax.fori_loop(0, laps, functools.partial(finish_lap, g), 0)

    order = [(g, lap) for g in range(GROUPS) for lap in range(laps)]
    for n in range(len(order) + 1):
        if n < len(order):
            if order[n][1] == 0:
                for load in first_loads[order[n][0]]:
                    load.wait()
            forward_states(*order[n])
        if n == 1:
            pl.semaphore_wait(barrier, heads - 1 + planes - 1)
        if n > 0:
            forward_sends(*order[n - 1])
    for load in late_loads:
        load.start()

    col_doc = doc_of(start + lax.broadcasted_iota(jnp.int32, (DH, DH), 1))
    causal = lax.broadcasted_iota(jnp.int32, (DH, DH), 0) >= lax.broadcasted_iota(
        jnp.int32, (DH, DH), 1
    )
    visible_ref[...] = jnp.where(causal & (row_doc == col_doc), 1.0, 0.0).astype(F32)
    rows_ref[0] = jnp.where(row_doc == doc_of(start), 1.0, 0.0).astype(F32)

    plane_start = z * (heads * DH)
    plane_first = doc_of(plane_start)
    plane_last = doc_of(plane_start + heads * DH - 1)

    def weigh(i, carry):
        begin = plane_start + i * DH
        before, first = doc_of(begin - 1), doc_of(begin)
        last, after = doc_of(begin + DH - 1), doc_of(begin + DH)
        weight_ref[0, i] = equal(last, plane_last)
        weight_ref[1, i] = equal(last, before)
        weight_ref[2, i] = equal(first, before)
        weight_ref[3, i] = equal(first, plane_first)
        weight_ref[4, i] = equal(first, after)
        weight_ref[5, i] = equal(last, after)
        return carry

    lax.fori_loop(0, heads, weigh, 0)
    before_plane, after_plane = doc_of(plane_start - 1), doc_of(plane_start + heads * DH)
    for n in range(1, reach + 1):
        lower = equal(doc_of((z - n + 1) * (heads * DH) - 1), before_plane)
        upper = equal(doc_of((z + n) * (heads * DH)), after_plane)
        zweight_ref[0, n - 1] = jnp.where(z >= n, lower, 0.0)
        zweight_ref[1, n - 1] = jnp.where(z + n < planes, upper, 0.0)

    for load in late_loads:
        load.wait()
    steps = {
        "L": local_forward,
        "T": functools.partial(sum_up, 0),
        "P": functools.partial(scan, 0),
        "A": attend,
        "M": local_back,
        "U": functools.partial(sum_up, 1),
        "Q": functools.partial(scan, 1),
        "F": finish,
    }
    for n in range(0, len(SCHEDULE), 2):
        steps[SCHEDULE[n]](int(SCHEDULE[n + 1]))
    for way in range(2):
        for n in range(2):
            sent = state_out.at[way, pl.ds(0, heads - 1)]
            pltpu.make_async_copy(sent, sent, send_sem.at[way, n]).wait()
        for n in range(1, reach + 1):
            pltpu.make_async_copy(total_out.at[way], total_out.at[way], zsend_sem.at[way]).wait()


def write_out(*refs):
    sources, targets, sem = refs[:4], refs[4:8], refs[8]
    step = sources[0].shape[0] // WRITES
    copies = [
        pltpu.make_async_copy(
            sources[n].at[pl.ds(m * step, step)], targets[n].at[pl.ds(m * step, step)], sem.at[n, m]
        )
        for n in range(4)
        for m in range(WRITES)
    ]
    for copy in copies:
        copy.start()
    for copy in copies:
        copy.wait()


def solution(mesh):
    seq_axis, head_axis = mesh.shape["seq"], mesh.shape["head"]

    def local(queries, keys, values, out_grad, doc_lengths):
        rows, width = queries.shape
        heads = width // DH
        plane_seq = heads // head_axis
        planes = seq_axis // plane_seq
        reach = min(planes - 1, -(-DOC_MOST // (heads * DH)))
        cfg = (heads, plane_seq, head_axis, planes, reach)
        flat = [pltpu.VMEM((rows, width), BF16)] * 4
        per_head = [pltpu.VMEM((heads, DH, DH), BF16)] * 5
        wide = [pltpu.VMEM((heads, DH, DH), F32)] * 3
        out = jax.ShapeDtypeStruct((rows, width), BF16)
        hbm = pl.BlockSpec(memory_space=pl.ANY)
        parts = pl.pallas_call(
            functools.partial(kernel, cfg),
            out_shape=(pltpu.VMEM((rows, width), BF16),) * 4,
            in_specs=[pl.BlockSpec(memory_space=pltpu.SMEM)] + [hbm] * 4,
            out_specs=(pl.BlockSpec(memory_space=pltpu.VMEM),) * 4,
            scratch_shapes=flat
            + per_head
            + [pltpu.VMEM((heads, DH, DH), BF16)] * 2
            + [pltpu.VMEM((heads, DH, DH), F32)]
            + wide
            + [
                pltpu.VMEM((2, heads, DH, DH), BF16),
                pltpu.VMEM((2, GROUPS, heads, DH // GROUPS, DH), BF16),
                pltpu.VMEM((2, GROUPS, heads, DH // GROUPS, DH), BF16),
                pltpu.VMEM((2, heads, DH, DH), BF16),
                pltpu.VMEM((2, GROUPS, DH // GROUPS, DH), BF16),
                pltpu.VMEM((2, GROUPS, reach, DH // GROUPS, DH), BF16),
                pltpu.VMEM((DH, DH), F32),
                pltpu.VMEM((2, DH, DH), F32),
                pltpu.SMEM((6, heads), F32),
                pltpu.SMEM((2, reach), F32),
                pltpu.SemaphoreType.DMA((2, 2)),
                pltpu.SemaphoreType.DMA((2, GROUPS)),
                pltpu.SemaphoreType.DMA((2, heads)),
                pltpu.SemaphoreType.DMA((2,)),
                pltpu.SemaphoreType.DMA((2, GROUPS, reach)),
                pltpu.SemaphoreType.DMA((2 + 2 * GROUPS,)),
            ],
            compiler_params=pltpu.CompilerParams(
                collective_id=0, has_side_effects=True, vmem_limit_bytes=KERNEL_VMEM_KIB << 10
            ),
        )(doc_lengths, queries, keys, values, out_grad)
        return pl.pallas_call(
            write_out,
            out_shape=(out,) * 4,
            in_specs=[pl.BlockSpec(memory_space=pltpu.VMEM)] * 4,
            out_specs=(hbm,) * 4,
            scratch_shapes=[pltpu.SemaphoreType.DMA((4, WRITES))],
            compiler_params=pltpu.CompilerParams(vmem_limit_bytes=16 << 20),
        )(*parts)

    return jax.shard_map(
        local,
        mesh=mesh,
        in_specs=(P(("seq", "head"), None),) * 4 + (P(),),
        out_specs=(P(("seq", "head"), None),) * 4,
        check_vma=False,
    )
```
